256 devices in a mesh: dp: 64 (over x, z_lo, y, core), tensor: 4 (over z_hi).
Axes of the slice: x: 4, y: 4, z: 8 (z_hi: 4, z_lo: 2; z = z_hi * 2 + z_lo), core: 2. Of those that a mesh axis runs over, the one named last changes fastest.
Arguments:
- activations: bfloat16 [1, 8192, 4096], P(None, ('dp', 'tensor')), may hold values from -6 to 6
- out_grad: bfloat16 [1, 8192, 512], P(None, 'dp', 'tensor'), may hold values from -0.5 to 0.5
- value_weight: bfloat16 [1, 512, 4096], P(None, 'tensor'), may hold values from -6 to 6
- error_feedback: bfloat16 [1, 64, 512, 4096], P(None, 'dp', 'tensor'), may hold values from -8 to 8
- warm_right: bfloat16 [1, 4, 4096, 32], P(None, 'tensor'), may hold values from -6 to 6
Outputs:
- new_error: bfloat16 [1, 64, 512, 4096], P(None, 'dp', 'tensor')
- left_basis: float32 [1, 512, 32], P(None, 'tensor')
- right_factor: bfloat16 [1, 4, 4096, 32], P(None, 'tensor')
- input_grad: bfloat16 [1, 8192, 4096], P(None, ('dp', 'tensor'))
The draws below stay inside these ranges and needn't reach their ends.
All inputs are finite; a program needn't handle non-finite values.
Results may differ from the reference program's by a relative error of at most 0.00065.
Values may be sent and summed in bfloat16 or wider, within the bound.
No kernel may reach another device: no remote copies, remote signals or barrier semaphores. Data moves between devices by JAX's collectives and lax.ppermute only.
A program may use at most 64 MiB of HBM per device.

```python
import jax
import jax.numpy as jnp
from jax import lax

D = 4096
HEAD = 128
R = 32
LAYERS = 1
VALUE_HEADS = 4
VALUE_WIDTH = 512
REP_TOK = 128
TOKENS = 8192
N_DP = 64


def draw_error_feedback(key, part):
    shared_key = jax.random.fold_in(key, 11)
    own_key = jax.random.fold_in(key, 12)
    shared = jax.random.normal(shared_key, (LAYERS, 1, VALUE_WIDTH, D), jnp.float32)
    own = jax.random.normal(own_key, (LAYERS, N_DP, VALUE_WIDTH, D), jnp.float32)
    values = shared + 0.5 * own
    return jnp.clip(values, -8.0, 8.0).astype(jnp.bfloat16)


def block_scale(rng, dims, shards, low, high):
    def one(position, parts):
        steps = jax.random.uniform(jax.random.fold_in(jax.random.fold_in(rng, 6), position), (parts,), jnp.float32, low / len(shards), high / len(shards))
        return jnp.repeat(jnp.exp(steps), dims[position] // parts).reshape((-1,) + (1,) * (len(dims) - position - 1))

    level = one(*shards[0])
    for cut in shards[1:]:
        level = level * one(*cut)
    return level


def scatter_about(stream_key, shape, width, limit, pieces=(), dtype=jnp.bfloat16):
    entries = width * jax.random.normal(stream_key, shape, jnp.float32)
    if pieces:
        entries = entries * block_scale(stream_key, shape, pieces, -0.22, 0.18)
    return jnp.clip(entries, -limit, limit).astype(dtype)


def setup_inputs(seed: int = 0) -> dict:
    arg_keys = jax.random.split(jax.random.key(seed), 6)
    activations = scatter_about(arg_keys[0], (LAYERS, TOKENS, D), 1.0, 6.0, ((1, 256),))
    out_grad = scatter_about(arg_keys[1], (LAYERS, TOKENS, VALUE_WIDTH), REP_TOK ** -0.5, 0.5, ((1, 64), (2, 4)))
    value_weight = scatter_about(arg_keys[2], (LAYERS, VALUE_WIDTH, D), 1.0, 6.0, ((1, 4),))
    error_feedback = draw_error_feedback(jax.random.fold_in(arg_keys[5], 71), 0)
    warm_right = scatter_about(arg_keys[4], (LAYERS, VALUE_HEADS, D, R), 1.0, 6.0, ((1, 4),))
    return dict(activations=activations, out_grad=out_grad, value_weight=value_weight, error_feedback=error_feedback, warm_right=warm_right)


HIGH = lax.Precision.HIGHEST

def orthonormal(left):
    gram = jnp.einsum('bhk,bhj->bkj', left, left, precision=HIGH)
    lower = jnp.linalg.cholesky(gram)
    return lax.linalg.triangular_solve(lower, left, left_side=False, lower=True, transpose_a=True)

def reference(activations, out_grad, value_weight, error_feedback, warm_right):
    errors = []
    bases = []
    rights = []
    inputs = []
    for layer in range(LAYERS):
        tokens = activations[layer].reshape(N_DP, REP_TOK, D).astype(jnp.float32)
        grads = out_grad[layer].reshape(N_DP, REP_TOK, VALUE_WIDTH).astype(jnp.float32)
        weight_grad = jnp.einsum('rtk,rtd->rkd', grads, tokens, precision=HIGH)
        merged = weight_grad + error_feedback[layer].astype(jnp.float32)
        blocks = merged.reshape(N_DP, VALUE_HEADS, HEAD, D)
        warm = warm_right[layer].astype(jnp.float32)
        left = jnp.einsum('rbhd,bdk->bhk', blocks, warm, precision=HIGH) / N_DP
        basis = orthonormal(left)
        right = jnp.einsum('rbhd,bhk->bdk', blocks, basis, precision=HIGH) / N_DP
        approx = jnp.einsum('bhk,bdk->bhd', basis, right, precision=HIGH)
        residual = (blocks - approx[None]).reshape(N_DP, VALUE_WIDTH, D)
        errors.append(residual.astype(jnp.bfloat16))
        bases.append(basis.reshape(VALUE_WIDTH, R))
        rights.append(right.astype(jnp.bfloat16))
        inputs.append(jnp.dot(out_grad[layer].astype(jnp.float32), value_weight[layer].astype(jnp.float32), preferred_element_type=jnp.float32).astype(jnp.bfloat16))
    return (jnp.stack(errors), jnp.stack(bases), jnp.stack(rights), jnp.stack(inputs))
```

```python
import jax
import jax.numpy as jnp
from jax import lax
from jax.experimental import pallas as pl
from jax.experimental.pallas import tpu as pltpu
from jax.sharding import Mesh
from jax.sharding import PartitionSpec as P

F32 = jnp.float32
BF16 = jnp.bfloat16
HIGH = lax.Precision.HIGHEST
CHIPS = ("x", "zl", "y")
DP = ("x", "zl", "y", "core")
EVERY = DP + ("t",)

TENSOR = 4
REPLICAS = 64
WIDE = 4096
HEAD = 128
RANK = 32
HALF = RANK // 2
OWN = 32
PART = WIDE // TENSOR
N_CHIPS = REPLICAS // 2
STEP = 512
NT = (((1,), (1,)), ((), ()))


def split3(x):
    hi = x.astype(BF16)
    rest = x - hi.astype(F32)
    mid = rest.astype(BF16)
    low = (rest - mid.astype(F32)).astype(BF16)
    return (hi, mid, low)


def split2(x):
    hi = x.astype(BF16)
    return (hi, (x - hi.astype(F32)).astype(BF16))


def turned(ref, t):
    blocks = [ref[pl.ds(((t - k + TENSOR) % TENSOR) * OWN, OWN), :] for k in range(TENSOR)]
    return jnp.concatenate(blocks, axis=0)


def call(kernel, outs, scratch=(), flops=10**6, moved=10**6):
    vmem = pl.BlockSpec(memory_space=pltpu.VMEM)

    def run(*args):
        return pl.pallas_call(
            kernel,
            out_shape=[jax.ShapeDtypeStruct(s, d) for s, d in outs],
            in_specs=[vmem] * len(args),
            out_specs=[vmem] * len(outs),
            scratch_shapes=list(scratch),
            compiler_params=pltpu.CompilerParams(vmem_limit_bytes=40 * 2**20),
            cost_estimate=pl.CostEstimate(flops=flops, bytes_accessed=moved, transcendentals=0),
        )(*args)

    return run


def pack_kernel(w, og, *sends):
    t, core = lax.axis_index("t"), lax.axis_index("core")
    rows = pl.ds(pl.multiple_of(core * 64, 64), 64)
    for k, send in enumerate(sends, 1):
        target = lax.rem(t + k, TENSOR)
        send[0:64, :] = w[rows, pl.ds(pl.multiple_of(target * PART, PART), PART)]
        for m in range(8):
            send[64:80, 128 * m : 128 * m + 128] = og[16 * m : 16 * m + 16, :]


def left_kernel(a0, a1, a2, a3, og, ef, warm, keep, send, held):
    t, core = lax.axis_index("t"), lax.axis_index("core")
    lines = warm[...]
    ogp = turned(og, t)
    inner = jnp.concatenate(
        [lax.dot_general(lines, a[...], NT, preferred_element_type=F32) for a in (a0, a1, a2, a3)],
        axis=1,
    )
    parts = jnp.concatenate(split3(inner), axis=0)
    prod = jnp.dot(parts, ogp, preferred_element_type=F32)
    fed = lax.dot_general(lines, ef[...], NT, preferred_element_type=F32)
    held[...] = prod[0:RANK] + prod[RANK : 2 * RANK] + prod[2 * RANK :] + fed
    keep[...] = held[pl.ds(pl.multiple_of(core * HALF, HALF), HALF), :]
    send[...] = held[pl.ds(pl.multiple_of((1 - core) * HALF, HALF), HALF), :]


def basis_kernel(lown, loth, a0, a1, a2, a3, og, ef, qt, keep, send, held, heldo):
    t, core = lax.axis_index("t"), lax.axis_index("core")
    mine = pl.ds(pl.multiple_of(core * HALF, HALF), HALF)
    other = pl.ds(pl.multiple_of((1 - core) * HALF, HALF), HALF)
    held[mine, :] = lown[...]
    held[other, :] = loth[...]
    left = held[...]
    gram = lax.dot_general(left, left, NT, precision=HIGH, preferred_element_type=F32)
    row = lax.broadcasted_iota(jnp.int32, (RANK, 1), 0)
    for k in range(RANK - 1):
        scale = 1.0 / gram[k : k + 1, k : k + 1]
        factor = jnp.where(row > k, gram[:, k : k + 1] * scale, 0.0)
        pivot_g, pivot_l = gram[k : k + 1, :], left[k : k + 1, :]
        gram = gram - factor * pivot_g
        left = left - factor * pivot_l
    eye = row == lax.broadcasted_iota(jnp.int32, (RANK, RANK), 1)
    diagonal = jnp.sum(jnp.where(eye, gram, 0.0), axis=1, keepdims=True)
    basis = left * (1.0 / jnp.sqrt(diagonal))
    qt[...] = basis
    ogp = turned(og, t)
    prod = lax.dot_general(
        jnp.concatenate(split3(basis), axis=0), ogp, NT, preferred_element_type=F32
    )
    held[...] = basis
    heldo[...] = prod[0:RANK] + prod[RANK : 2 * RANK] + prod[2 * RANK :]
    q = jnp.concatenate([held[mine, :], held[other, :]], axis=0)
    qo = jnp.concatenate([heldo[mine, :], heldo[other, :]], axis=0)
    lhs = jnp.concatenate(
        [jnp.concatenate(split3(qo), axis=0), jnp.concatenate(split3(q), axis=0)], axis=1
    )
    for c in range(0, WIDE, STEP):
        cols = slice(c, c + STEP)
        rhs = jnp.concatenate([a[:, cols] for a in (a0, a1, a2, a3, ef)], axis=0)
        p = jnp.dot(lhs, rhs, preferred_element_type=F32)
        r = p[0:RANK] + p[RANK : 2 * RANK] + p[2 * RANK :]
        for j in range(STEP // 128):
            chip = c // 128 + j
            keep[chip] = r[0:HALF, 128 * j : 128 * j + 128]
            send[chip] = r[HALF:, 128 * j : 128 * j + 128]


def spread_kernel(pieces, out):
    total = jnp.sum(pieces[...], axis=0) * (1.0 / REPLICAS)
    out[...] = jnp.broadcast_to(total[None], out.shape)


def finish_kernel(rown, roth, qt, og, a0, a1, a2, a3, ef, i0, i1, i2, i3, err, fac, igrad, held):
    t, core = lax.axis_index("t"), lax.axis_index("core")
    mine = pl.ds(pl.multiple_of(core * HALF, HALF), HALF)
    other = pl.ds(pl.multiple_of((1 - core) * HALF, HALF), HALF)
    for k, block in enumerate((i0, i1, i2, i3)):
        source = lax.rem(t - k + TENSOR, TENSOR)
        igrad[:, pl.ds(pl.multiple_of(source * PART, PART), PART)] = block[...]
    q = jnp.concatenate([qt[mine, :], qt[other, :]], axis=0)
    hi, mid = split2(q)
    hi, mid = hi.astype(F32), mid.astype(F32)
    ogp = turned(og, t).astype(F32)
    lhs = jnp.concatenate([ogp, -hi, -hi, -mid, -mid], axis=0).T.astype(BF16)
    for c in range(0, WIDE, STEP):
        cols = slice(c, c + STEP)
        ro = jnp.concatenate([rown[c // 128 + j] for j in range(STEP // 128)], axis=1)
        rt = jnp.concatenate([roth[c // 128 + j] for j in range(STEP // 128)], axis=1)
        fac[mine, cols] = ro.astype(BF16)
        fac[other, cols] = rt.astype(BF16)
        rhi, rmid = split2(jnp.concatenate([ro, rt], axis=0))
        rhs = jnp.concatenate([a[:, cols] for a in (a0, a1, a2, a3)] + [rhi, rmid, rhi, rmid], axis=0)
        total = jnp.dot(lhs, rhs, preferred_element_type=F32) + ef[:, cols].astype(F32)
        err[:, cols] = total.astype(BF16)


def input_kernel(w, og, r1, r2, r3, e1, e2, e3, o0, o1, o2, o3, weights, feats):
    t, core = lax.axis_index("t"), lax.axis_index("core")
    weights[0:128, :] = w[:, pl.ds(pl.multiple_of(t * PART, PART), PART)]
    feats[:, 0:128] = og[...]
    for k, (r, e) in enumerate(((r1, e1), (r2, e2), (r3, e3)), 1):
        weights[pl.ds(pl.multiple_of(128 * k + 64 * core, 64), 64), :] = r[0:64, :]
        weights[pl.ds(pl.multiple_of(128 * k + 64 * (1 - core), 64), 64), :] = e[0:64, :]
        for m in range(8):
            feats[16 * m : 16 * m + 16, 128 * k : 128 * k + 128] = r[64:80, 128 * m : 128 * m + 128]
    for k, out in enumerate((o0, o1, o2, o3)):
        target = lax.rem(t + k, TENSOR)
        rows = feats[pl.ds(pl.multiple_of(target * OWN, OWN), OWN), :]
        out[...] = jnp.dot(rows, weights[...], preferred_element_type=F32).astype(BF16)


def moved(x, k):
    return lax.ppermute(x, "t", [(i, (i + k) % TENSOR) for i in range(TENSOR)])


def swapped(x):
    return lax.ppermute(x, "core", [(0, 1), (1, 0)])


def exchanged(x):
    return lax.all_to_all(x, CHIPS, 0, 0, tiled=True)


def local(activations, out_grad, value_weight, error_feedback, warm_right):
    act, og, weight = activations[0], out_grad[0], value_weight[0]
    ef = error_feedback[0, 0]
    warm = warm_right[0, 0].T

    acts = [act] + [moved(act, k) for k in (1, 2, 3)]
    packed = ((OWN * 2 + 16, PART), BF16)
    sends = call(pack_kernel, [packed] * 3)(weight, og)

    half = ((HALF, HEAD), F32)
    left_keep, left_send = call(
        left_kernel, [half, half], [pltpu.VMEM((RANK, HEAD), F32)], flops=10**8, moved=3 * 10**6
    )(*acts, og, ef, warm)

    sends, left_send = lax.optimization_barrier((sends, left_send))
    got = [moved(s, k) for k, s in zip((1, 2, 3), sends)]

    left_half = left_keep + swapped(left_send)
    pieces = exchanged(jnp.broadcast_to(left_half[None], (N_CHIPS, HALF, HEAD)))
    left_own = jnp.sum(pieces, axis=0)
    left_other = swapped(left_own)
    left_other, got = lax.optimization_barrier((left_other, got))

    traded = [swapped(g) for g in got]
    block = ((N_CHIPS, HALF, 128), F32)
    basis, right_keep, right_send = call(
        basis_kernel,
        [((RANK, HEAD), F32), block, block],
        [pltpu.VMEM((RANK, HEAD), F32), pltpu.VMEM((RANK, HEAD), F32)],
        flops=10**8,
        moved=3 * 10**6,
    )(left_own, left_other, *acts, og, ef)

    outs = call(
        input_kernel,
        [((OWN, PART), BF16)] * 4,
        [pltpu.VMEM((512, PART), BF16), pltpu.VMEM((128, 512), BF16)],
        flops=2 * 10**8,
        moved=2 * 10**6,
    )(weight, og, *got, *traded)
    inputs = [outs[0]] + [moved(o, k) for k, o in zip((1, 2, 3), outs[1:])]

    pieces = exchanged(right_keep + swapped(right_send))
    pieces, outs = lax.optimization_barrier((pieces, outs))
    (mean,) = call(spread_kernel, [block])(pieces)
    right_own = exchanged(mean)
    right_own, inputs = lax.optimization_barrier((right_own, inputs))
    right_other = swapped(right_own)

    err, fac, igrad = call(
        finish_kernel,
        [((HEAD, WIDE), BF16), ((RANK, WIDE), BF16), ((OWN, WIDE), BF16)],
        [pltpu.VMEM((RANK, HEAD), F32)],
        flops=3 * 10**8,
        moved=5 * 10**6,
    )(right_own, right_other, basis, og, *acts, ef, *inputs)

    return (err[None, None], basis.T[None], fac.T[None, None], igrad[None])


def solution(mesh):
    parted = Mesh(
        mesh.devices.reshape(4, 2, 4, 2, 4), EVERY
    )
    return jax.shard_map(
        local,
        mesh=parted,
        in_specs=(
            P(None, EVERY, None),
            P(None, DP, "t"),
            P(None, "t", None),
            P(None, DP, "t", None),
            P(None, "t", None, None),
        ),
        out_specs=(
            P(None, DP, "t", None),
            P(None, "t", None),
            P(None, "t", None, None),
            P(None, EVERY, None),
        ),
        check_vma=False,
    )
```

```python
import jax
import jax.numpy as jnp
from jax import lax
from jax.experimental import pallas as pl
from jax.experimental.pallas import tpu as pltpu
from jax.sharding import Mesh
from jax.sharding import PartitionSpec as P

F32 = jnp.float32
BF16 = jnp.bfloat16
HIGH = lax.Precision.HIGHEST
CHIPS = ("x", "zl", "y")
DP = ("x", "zl", "y", "core")
EVERY = DP + ("t",)

TENSOR = 4
REPLICAS = 64
WIDE = 4096
HEAD = 128
RANK = 32
HALF = RANK // 2
OWN = 32
PART = WIDE // TENSOR
N_CHIPS = REPLICAS // 2
GROUP = 8
STEP = 512
NT = (((1,), (1,)), ((), ()))


def split3(x):
    hi = x.astype(BF16)
    rest = x - hi.astype(F32)
    mid = rest.astype(BF16)
    low = (rest - mid.astype(F32)).astype(BF16)
    return (hi, mid, low)


def split2(x):
    hi = x.astype(BF16)
    return (hi, (x - hi.astype(F32)).astype(BF16))


def turned(ref, t):
    blocks = [ref[pl.ds(((t - k + TENSOR) % TENSOR) * OWN, OWN), :] for k in range(TENSOR)]
    return jnp.concatenate(blocks, axis=0)


def call(kernel, outs, scratch=(), flops=10**6, moved=10**6):
    vmem = pl.BlockSpec(memory_space=pltpu.VMEM)

    def run(*args):
        return pl.pallas_call(
            kernel,
            out_shape=[jax.ShapeDtypeStruct(s, d) for s, d in outs],
            in_specs=[vmem] * len(args),
            out_specs=[vmem] * len(outs),
            scratch_shapes=list(scratch),
            compiler_params=pltpu.CompilerParams(vmem_limit_bytes=40 * 2**20),
            cost_estimate=pl.CostEstimate(flops=flops, bytes_accessed=moved, transcendentals=0),
        )(*args)

    return run


def early_kernel(w, og, a0, ef, warm, packed, inner, fed, lines):
    t, core = lax.axis_index("t"), lax.axis_index("core")
    rows = pl.ds(pl.multiple_of(core * 64, 64), 64)
    for target in range(TENSOR):
        packed[target, 0:64, :] = w[rows, target * PART : target * PART + PART]
        for m in range(8):
            packed[target, 64:80, 128 * m : 128 * m + 128] = og[16 * m : 16 * m + 16, :]
    lines[...] = warm[...]
    inner[...] = lax.dot_general(warm[...], a0[...], NT, preferred_element_type=F32)
    fed[...] = lax.dot_general(warm[...], ef[...], NT, preferred_element_type=F32)


def left_kernel(a1, a2, a3, og, lines, inner0, fed, out):
    t = lax.axis_index("t")
    ogp = turned(og, t)
    rest = [
        lax.dot_general(lines[...], a[...], NT, preferred_element_type=F32) for a in (a1, a2, a3)
    ]
    inner = jnp.concatenate([inner0[...]] + rest, axis=1)
    prod = jnp.dot(jnp.concatenate(split3(inner), axis=0), ogp, preferred_element_type=F32)
    left = prod[0:RANK] + prod[RANK : 2 * RANK] + prod[2 * RANK :] + fed[...]
    for k in range(GROUP):
        out[k] = left


def add_kernel(pieces, out):
    total = jnp.sum(pieces[...], axis=0)
    for k in range(GROUP):
        out[k] = total


def basis_kernel(lefts, a0, a1, a2, a3, og, ef, qt, keep, send, held, heldo):
    t, core = lax.axis_index("t"), lax.axis_index("core")
    mine = pl.ds(pl.multiple_of(core * HALF, HALF), HALF)
    other = pl.ds(pl.multiple_of((1 - core) * HALF, HALF), HALF)
    left = jnp.sum(lefts[...], axis=0)
    gram = lax.dot_general(left, left, NT, precision=HIGH, preferred_element_type=F32)
    row = lax.broadcasted_iota(jnp.int32, (RANK, 1), 0)
    for k in range(RANK - 1):
        scale = 1.0 / gram[k : k + 1, k : k + 1]
        factor = jnp.where(row > k, gram[:, k : k + 1] * scale, 0.0)
        pivot_g, pivot_l = gram[k : k + 1, :], left[k : k + 1, :]
        gram = gram - factor * pivot_g
        left = left - factor * pivot_l
    eye = row == lax.broadcasted_iota(jnp.int32, (RANK, RANK), 1)
    diagonal = jnp.sum(jnp.where(eye, gram, 0.0), axis=1, keepdims=True)
    basis = left * (1.0 / jnp.sqrt(diagonal))
    qt[...] = basis
    ogp = turned(og, t)
    prod = lax.dot_general(
        jnp.concatenate(split3(basis), axis=0), ogp, NT, preferred_element_type=F32
    )
    held[...] = basis
    heldo[...] = prod[0:RANK] + prod[RANK : 2 * RANK] + prod[2 * RANK :]
    q = jnp.concatenate([held[mine, :], held[other, :]], axis=0)
    qo = jnp.concatenate([heldo[mine, :], heldo[other, :]], axis=0)
    lhs = jnp.concatenate(
        [jnp.concatenate(split3(qo), axis=0), jnp.concatenate(split3(q), axis=0)], axis=1
    )
    for c in range(0, WIDE, STEP):
        cols = slice(c, c + STEP)
        rhs = jnp.concatenate([a[:, cols] for a in (a0, a1, a2, a3, ef)], axis=0)
        p = jnp.dot(lhs, rhs, preferred_element_type=F32)
        r = p[0:RANK] + p[RANK : 2 * RANK] + p[2 * RANK :]
        for j in range(STEP // 128):
            chip = c // 128 + j
            keep[chip] = r[0:HALF, 128 * j : 128 * j + 128]
            send[chip] = r[HALF:, 128 * j : 128 * j + 128]


def spread_kernel(pieces, out):
    total = jnp.sum(pieces[...], axis=0) * (1.0 / REPLICAS)
    out[...] = jnp.broadcast_to(total[None], out.shape)


def finish_kernel(rown, roth, qt, og, a0, a1, a2, a3, ef, parts, err, fac, igrad):
    t, core = lax.axis_index("t"), lax.axis_index("core")
    mine = pl.ds(pl.multiple_of(core * HALF, HALF), HALF)
    other = pl.ds(pl.multiple_of((1 - core) * HALF, HALF), HALF)
    for source in range(TENSOR):
        igrad[:, source * PART : source * PART + PART] = parts[source]
    q = jnp.concatenate([qt[mine, :], qt[other, :]], axis=0)
    hi, mid = split2(q)
    hi, mid = hi.astype(F32), mid.astype(F32)
    ogp = turned(og, t).astype(F32)
    lhs = jnp.concatenate([ogp, -hi, -hi, -mid, -mid], axis=0).T.astype(BF16)
    for c in range(0, WIDE, STEP):
        cols = slice(c, c + STEP)
        ro = jnp.concatenate([rown[c // 128 + j] for j in range(STEP // 128)], axis=1)
        rt = jnp.concatenate([roth[c // 128 + j] for j in range(STEP // 128)], axis=1)
        fac[mine, cols] = ro.astype(BF16)
        fac[other, cols] = rt.astype(BF16)
        rhi, rmid = split2(jnp.concatenate([ro, rt], axis=0))
        rhs = jnp.concatenate([a[:, cols] for a in (a0, a1, a2, a3)] + [rhi, rmid, rhi, rmid], axis=0)
        total = jnp.dot(lhs, rhs, preferred_element_type=F32) + ef[:, cols].astype(F32)
        err[:, cols] = total.astype(BF16)


def input_kernel(got, traded, outs, weights, feats):
    core = lax.axis_index("core")
    for k in range(TENSOR):
        weights[pl.ds(pl.multiple_of(128 * k + 64 * core, 64), 64), :] = got[k, 0:64, :]
        weights[pl.ds(pl.multiple_of(128 * k + 64 * (1 - core), 64), 64), :] = traded[k, 0:64, :]
        for m in range(8):
            feats[16 * m : 16 * m + 16, 128 * k : 128 * k + 128] = got[
                k, 64:80, 128 * m : 128 * m + 128
            ]
    total = jnp.dot(feats[...], weights[...], preferred_element_type=F32).astype(BF16)
    for k in range(TENSOR):
        outs[k] = total[OWN * k : OWN * k + OWN]


def moved(x, k):
    return lax.ppermute(x, "t", [(i, (i + k) % TENSOR) for i in range(TENSOR)])


def swapped(x):
    return lax.ppermute(x, "core", [(0, 1), (1, 0)])


def exchanged(x, axes):
    return lax.all_to_all(x, axes, 0, 0, tiled=True)


def local(activations, out_grad, value_weight, error_feedback, warm_right):
    act, og, weight = activations[0], out_grad[0], value_weight[0]
    ef = error_feedback[0, 0]
    warm = warm_right[0, 0].T

    acts = [act] + [moved(act, k) for k in (1, 2, 3)]
    packed, inner, fed, lines = call(
        early_kernel,
        [
            ((TENSOR, OWN * 2 + 16, PART), BF16),
            ((RANK, OWN), F32),
            ((RANK, HEAD), F32),
            ((RANK, WIDE), BF16),
        ],
        flops=5 * 10**7,
        moved=4 * 10**6,
    )(weight, og, act, ef, warm)

    group = ((GROUP, RANK, HEAD), F32)
    (left,) = call(left_kernel, [group], flops=5 * 10**7, moved=10**6)(
        *acts[1:], og, lines, inner, fed
    )
    left, packed = lax.optimization_barrier((left, packed))
    got = exchanged(packed, "t")
    (left,) = call(add_kernel, [group])(exchanged(left, ("y", "core")))
    left = exchanged(left, ("x", "zl"))

    block = ((N_CHIPS, HALF, 128), F32)
    basis, right_keep, right_send = call(
        basis_kernel,
        [((RANK, HEAD), F32), block, block],
        [pltpu.VMEM((RANK, HEAD), F32), pltpu.VMEM((RANK, HEAD), F32)],
        flops=10**8,
        moved=3 * 10**6,
    )(left, *acts, og, ef)

    pieces = exchanged(right_keep + swapped(right_send), CHIPS)
    pieces, got = lax.optimization_barrier((pieces, got))
    (mean,) = call(spread_kernel, [block])(pieces)

    (outs,) = call(
        input_kernel,
        [((TENSOR, OWN, PART), BF16)],
        [pltpu.VMEM((512, PART), BF16), pltpu.VMEM((128, 512), BF16)],
        flops=2 * 10**8,
        moved=2 * 10**6,
    )(got, swapped(got))
    mean, outs = lax.optimization_barrier((mean, outs))
    inputs = exchanged(outs, "t")

    right_own = exchanged(mean, CHIPS)
    right_other = swapped(right_own)

    err, fac, igrad = call(
        finish_kernel,
        [((HEAD, WIDE), BF16), ((RANK, WIDE), BF16), ((OWN, WIDE), BF16)],
        flops=3 * 10**8,
        moved=5 * 10**6,
    )(right_own, right_other, basis, og, *acts, ef, inputs)

    return (err[None, None], basis.T[None], fac.T[None, None], igrad[None])


def solution(mesh):
    parted = Mesh(
        mesh.devices.reshape(4, 2, 4, 2, 4), EVERY
    )
    return jax.shard_map(
        local,
        mesh=parted,
        in_specs=(
            P(None, EVERY, None),
            P(None, DP, "t"),
            P(None, "t", None),
            P(None, DP, "t", None),
            P(None, "t", None, None),
        ),
        out_specs=(
            P(None, DP, "t", None),
            P(None, "t", None),
            P(None, "t", None, None),
            P(None, EVERY, None),
        ),
        check_vma=False,
    )
```

```python
import jax
import jax.numpy as jnp
from jax import lax
from jax.experimental import pallas as pl
from jax.experimental.pallas import tpu as pltpu
from jax.sharding import Mesh
from jax.sharding import PartitionSpec as P

F32 = jnp.float32
BF16 = jnp.bfloat16
HIGH = lax.Precision.HIGHEST
CHIPS = ("x", "zl", "y")
DP = ("x", "zl", "y", "core")
EVERY = DP + ("t",)

TENSOR = 4
REPLICAS = 64
WIDE = 4096
HEAD = 128
RANK = 32
HALF = RANK // 2
OWN = 32
N_CHIPS = REPLICAS // 2
STEP = 512
NT = (((1,), (1,)), ((), ()))


def split3(x):
    hi = x.astype(BF16)
    rest = x - hi.astype(F32)
    mid = rest.astype(BF16)
    low = (rest - mid.astype(F32)).astype(BF16)
    return (hi, mid, low)


def split2(x):
    hi = x.astype(BF16)
    return (hi, (x - hi.astype(F32)).astype(BF16))


def turned(ref, t):
    blocks = [ref[pl.ds(((t - k + TENSOR) % TENSOR) * OWN, OWN), :] for k in range(TENSOR)]
    return jnp.concatenate(blocks, axis=0)


def call(kernel, outs, scratch=(), flops=10**6, moved=10**6):
    vmem = pl.BlockSpec(memory_space=pltpu.VMEM)

    def run(*args):
        return pl.pallas_call(
            kernel,
            out_shape=[jax.ShapeDtypeStruct(s, d) for s, d in outs],
            in_specs=[vmem] * len(args),
            out_specs=[vmem] * len(outs),
            scratch_shapes=list(scratch),
            compiler_params=pltpu.CompilerParams(vmem_limit_bytes=40 * 2**20),
            cost_estimate=pl.CostEstimate(flops=flops, bytes_accessed=moved, transcendentals=0),
        )(*args)

    return run


def early_kernel(w, og, a0, ef, warm, p0, p1, p2, p3, inner, fed, lines):
    t = lax.axis_index("t")
    lines[...] = warm[...]
    inner[...] = lax.dot_general(warm[...], a0[...], NT, preferred_element_type=F32)
    fed[...] = lax.dot_general(warm[...], ef[...], NT, preferred_element_type=F32)
    targets = jnp.concatenate(
        [og[pl.ds(lax.rem(t + k, TENSOR) * OWN, OWN), :] for k in range(TENSOR)], axis=0
    )
    for c in range(0, WIDE, STEP):
        share = jnp.dot(targets, w[:, c : c + STEP], preferred_element_type=F32)
        for k, out in enumerate((p0, p1, p2, p3)):
            out[:, c : c + STEP] = share[OWN * k : OWN * k + OWN]


def left_kernel(a1, a2, a3, og, lines, inner0, fed, keep, send, held):
    t, core = lax.axis_index("t"), lax.axis_index("core")
    ogp = turned(og, t)
    rest = [
        lax.dot_general(lines[...], a[...], NT, preferred_element_type=F32) for a in (a1, a2, a3)
    ]
    inner = jnp.concatenate([inner0[...]] + rest, axis=1)
    prod = jnp.dot(jnp.concatenate(split3(inner), axis=0), ogp, preferred_element_type=F32)
    held[...] = prod[0:RANK] + prod[RANK : 2 * RANK] + prod[2 * RANK :] + fed[...]
    keep[...] = held[pl.ds(pl.multiple_of(core * HALF, HALF), HALF), :]
    send[...] = held[pl.ds(pl.multiple_of((1 - core) * HALF, HALF), HALF), :]


def basis_kernel(lown, loth, a0, a1, a2, a3, og, ef, qt, keep, send, held, heldo):
    t, core = lax.axis_index("t"), lax.axis_index("core")
    mine = pl.ds(pl.multiple_of(core * HALF, HALF), HALF)
    other = pl.ds(pl.multiple_of((1 - core) * HALF, HALF), HALF)
    held[mine, :] = lown[...]
    held[other, :] = loth[...]
    left = held[...]
    gram = lax.dot_general(left, left, NT, precision=HIGH, preferred_element_type=F32)
    row = lax.broadcasted_iota(jnp.int32, (RANK, 1), 0)
    for k in range(RANK - 1):
        scale = 1.0 / gram[k : k + 1, k : k + 1]
        factor = jnp.where(row > k, gram[:, k : k + 1] * scale, 0.0)
        pivot_g, pivot_l = gram[k : k + 1, :], left[k : k + 1, :]
        gram = gram - factor * pivot_g
        left = left - factor * pivot_l
    eye = row == lax.broadcasted_iota(jnp.int32, (RANK, RANK), 1)
    diagonal = jnp.sum(jnp.where(eye, gram, 0.0), axis=1, keepdims=True)
    basis = left * (1.0 / jnp.sqrt(diagonal))
    qt[...] = basis
    ogp = turned(og, t)
    prod = lax.dot_general(
        jnp.concatenate(split3(basis), axis=0), ogp, NT, preferred_element_type=F32
    )
    held[...] = basis
    heldo[...] = prod[0:RANK] + prod[RANK : 2 * RANK] + prod[2 * RANK :]
    q = jnp.concatenate([held[mine, :], held[other, :]], axis=0)
    qo = jnp.concatenate([heldo[mine, :], heldo[other, :]], axis=0)
    lhs = jnp.concatenate(
        [jnp.concatenate(split3(qo), axis=0), jnp.concatenate(split3(q), axis=0)], axis=1
    )
    for c in range(0, WIDE, STEP):
        cols = slice(c, c + STEP)
        rhs = jnp.concatenate([a[:, cols] for a in (a0, a1, a2, a3, ef)], axis=0)
        p = jnp.dot(lhs, rhs, preferred_element_type=F32)
        r = p[0:RANK] + p[RANK : 2 * RANK] + p[2 * RANK :]
        for j in range(STEP // 128):
            chip = c // 128 + j
            keep[chip] = r[0:HALF, 128 * j : 128 * j + 128]
            send[chip] = r[HALF:, 128 * j : 128 * j + 128]


def spread_kernel(pieces, out):
    total = jnp.sum(pieces[...], axis=0) * (1.0 / REPLICAS)
    out[...] = jnp.broadcast_to(total[None], out.shape)


def finish_kernel(rown, roth, qt, og, a0, a1, a2, a3, ef, err, fac):
    t, core = lax.axis_index("t"), lax.axis_index("core")
    mine = pl.ds(pl.multiple_of(core * HALF, HALF), HALF)
    other = pl.ds(pl.multiple_of((1 - core) * HALF, HALF), HALF)
    q = jnp.concatenate([qt[mine, :], qt[other, :]], axis=0)
    hi, mid = split2(q)
    hi, mid = hi.astype(F32), mid.astype(F32)
    ogp = turned(og, t).astype(F32)
    lhs = jnp.concatenate([ogp, -hi, -hi, -mid, -mid], axis=0).T.astype(BF16)
    for c in range(0, WIDE, STEP):
        cols = slice(c, c + STEP)
        ro = jnp.concatenate([rown[c // 128 + j] for j in range(STEP // 128)], axis=1)
        rt = jnp.concatenate([roth[c // 128 + j] for j in range(STEP // 128)], axis=1)
        fac[mine, cols] = ro.astype(BF16)
        fac[other, cols] = rt.astype(BF16)
        rhi, rmid = split2(jnp.concatenate([ro, rt], axis=0))
        rhs = jnp.concatenate([a[:, cols] for a in (a0, a1, a2, a3)] + [rhi, rmid, rhi, rmid], axis=0)
        total = jnp.dot(lhs, rhs, preferred_element_type=F32) + ef[:, cols].astype(F32)
        err[:, cols] = total.astype(BF16)


def moved(x, k):
    return lax.ppermute(x, "t", [(i, (i + k) % TENSOR) for i in range(TENSOR)])


def swapped(x):
    return lax.ppermute(x, "core", [(0, 1), (1, 0)])


def exchanged(x, axes):
    return lax.all_to_all(x, axes, 0, 0, tiled=True)


def local(activations, out_grad, value_weight, error_feedback, warm_right):
    act, og, weight = activations[0], out_grad[0], value_weight[0]
    ef = error_feedback[0, 0]
    warm = warm_right[0, 0].T

    acts = [act] + [moved(act, k) for k in (1, 2, 3)]
    share = ((OWN, WIDE), F32)
    *shares, inner, fed, lines = call(
        early_kernel,
        [share] * 4 + [((RANK, OWN), F32), ((RANK, HEAD), F32), ((RANK, WIDE), BF16)],
        flops=2 * 10**8,
        moved=6 * 10**6,
    )(weight, og, act, ef, warm)

    half = ((HALF, HEAD), F32)
    left_keep, left_send = call(
        left_kernel, [half, half], [pltpu.VMEM((RANK, HEAD), F32)], flops=5 * 10**7, moved=10**6
    )(*acts[1:], og, lines, inner, fed)
    shares, left_send = lax.optimization_barrier((shares, left_send))
    near = [moved(shares[1], 1), moved(shares[3], 3)]

    left_half = left_keep + swapped(left_send)
    pieces = exchanged(jnp.broadcast_to(left_half[None], (N_CHIPS, HALF, HEAD)), CHIPS)
    left_own = jnp.sum(pieces, axis=0)
    left_other = swapped(left_own)

    block = ((N_CHIPS, HALF, 128), F32)
    basis, right_keep, right_send = call(
        basis_kernel,
        [((RANK, HEAD), F32), block, block],
        [pltpu.VMEM((RANK, HEAD), F32), pltpu.VMEM((RANK, HEAD), F32)],
        flops=10**8,
        moved=3 * 10**6,
    )(left_own, left_other, *acts, og, ef)

    right_send, near, far = lax.optimization_barrier((right_send, near, shares[2]))
    far = moved(far, 2)
    pieces = exchanged(right_keep + swapped(right_send), CHIPS)
    (mean,) = call(spread_kernel, [block])(pieces)
    right_own = exchanged(mean, CHIPS)
    right_other = swapped(right_own)

    err, fac = call(
        finish_kernel,
        [((HEAD, WIDE), BF16), ((RANK, WIDE), BF16)],
        flops=3 * 10**8,
        moved=5 * 10**6,
    )(right_own, right_other, basis, og, *acts, ef)
    igrad = (shares[0] + near[0] + near[1] + far).astype(BF16)

    return (err[None, None], basis.T[None], fac.T[None, None], igrad[None])


def solution(mesh):
    parted = Mesh(
        mesh.devices.reshape(4, 2, 4, 2, 4), EVERY
    )
    return jax.shard_map(
        local,
        mesh=parted,
        in_specs=(
            P(None, EVERY, None),
            P(None, DP, "t"),
            P(None, "t", None),
            P(None, DP, "t", None),
            P(None, "t", None, None),
        ),
        out_specs=(
            P(None, DP, "t", None),
            P(None, "t", None),
            P(None, "t", None, None),
            P(None, EVERY, None),
        ),
        check_vma=False,
    )
```

```python
import jax
import jax.numpy as jnp
from jax import lax
from jax.experimental import pallas as pl
from jax.experimental.pallas import tpu as pltpu
from jax.sharding import Mesh
from jax.sharding import PartitionSpec as P

F32 = jnp.float32
BF16 = jnp.bfloat16
HIGH = lax.Precision.HIGHEST
CHIPS = ("x", "zl", "y")
DP = ("x", "zl", "y", "core")
EVERY = DP + ("t",)

TENSOR = 4
REPLICAS = 64
WIDE = 4096
HEAD = 128
RANK = 32
HALF = RANK // 2
OWN = 32
CUT = 16
PART = WIDE // TENSOR
N_CHIPS = REPLICAS // 2
STEP = 512
NT = (((1,), (1,)), ((), ()))


def split3(x):
    hi = x.astype(BF16)
    rest = x - hi.astype(F32)
    mid = rest.astype(BF16)
    low = (rest - mid.astype(F32)).astype(BF16)
    return (hi, mid, low)


def split2(x):
    hi = x.astype(BF16)
    return (hi, (x - hi.astype(F32)).astype(BF16))


def turned(ref, t):
    blocks = [ref[pl.ds(((t - k + TENSOR) % TENSOR) * OWN, OWN), :] for k in range(TENSOR)]
    return jnp.concatenate(blocks, axis=0)


def call(kernel, outs, scratch=(), flops=10**6, moved=10**6):
    vmem = pl.BlockSpec(memory_space=pltpu.VMEM)

    def run(*args):
        return pl.pallas_call(
            kernel,
            out_shape=[jax.ShapeDtypeStruct(s, d) for s, d in outs],
            in_specs=[vmem] * len(args),
            out_specs=[vmem] * len(outs),
            scratch_shapes=list(scratch),
            compiler_params=pltpu.CompilerParams(vmem_limit_bytes=40 * 2**20),
            cost_estimate=pl.CostEstimate(flops=flops, bytes_accessed=moved, transcendentals=0),
        )(*args)

    return run


def pack_kernel(w, og, *sends):
    t, y, core = lax.axis_index("t"), lax.axis_index("y"), lax.axis_index("core")
    rows = pl.ds(pl.multiple_of((2 * y + core) * CUT, CUT), CUT)
    for k, send in enumerate(sends, 1):
        target = lax.rem(t + k, TENSOR)
        send[0:CUT, :] = w[rows, pl.ds(pl.multiple_of(target * PART, PART), PART)]
        for m in range(8):
            send[CUT : 2 * CUT, 128 * m : 128 * m + 128] = og[16 * m : 16 * m + 16, :]


def early_kernel(a0, ef, warm, inner, fed, lines):
    lines[...] = warm[...]
    inner[...] = lax.dot_general(warm[...], a0[...], NT, preferred_element_type=F32)
    fed[...] = lax.dot_general(warm[...], ef[...], NT, preferred_element_type=F32)


def left_kernel(a1, a2, a3, og, lines, inner0, fed, keep, send, held):
    t, core = lax.axis_index("t"), lax.axis_index("core")
    ogp = turned(og, t)
    rest = [
        lax.dot_general(lines[...], a[...], NT, preferred_element_type=F32) for a in (a1, a2, a3)
    ]
    inner = jnp.concatenate([inner0[...]] + rest, axis=1)
    prod = jnp.dot(jnp.concatenate(split3(inner), axis=0), ogp, preferred_element_type=F32)
    held[...] = prod[0:RANK] + prod[RANK : 2 * RANK] + prod[2 * RANK :] + fed[...]
    keep[...] = held[pl.ds(pl.multiple_of(core * HALF, HALF), HALF), :]
    send[...] = held[pl.ds(pl.multiple_of((1 - core) * HALF, HALF), HALF), :]


def basis_kernel(lown, loth, a0, a1, a2, a3, og, ef, qt, keep, send, held, heldo):
    t, core = lax.axis_index("t"), lax.axis_index("core")
    mine = pl.ds(pl.multiple_of(core * HALF, HALF), HALF)
    other = pl.ds(pl.multiple_of((1 - core) * HALF, HALF), HALF)
    held[mine, :] = lown[...]
    held[other, :] = loth[...]
    left = held[...]
    gram = lax.dot_general(left, left, NT, precision=HIGH, preferred_element_type=F32)
    row = lax.broadcasted_iota(jnp.int32, (RANK, 1), 0)
    for k in range(RANK - 1):
        scale = 1.0 / gram[k : k + 1, k : k + 1]
        factor = jnp.where(row > k, gram[:, k : k + 1] * scale, 0.0)
        pivot_g, pivot_l = gram[k : k + 1, :], left[k : k + 1, :]
        gram = gram - factor * pivot_g
        left = left - factor * pivot_l
    eye = row == lax.broadcasted_iota(jnp.int32, (RANK, RANK), 1)
    diagonal = jnp.sum(jnp.where(eye, gram, 0.0), axis=1, keepdims=True)
    basis = left * (1.0 / jnp.sqrt(diagonal))
    qt[...] = basis
    ogp = turned(og, t)
    prod = lax.dot_general(
        jnp.concatenate(split3(basis), axis=0), ogp, NT, preferred_element_type=F32
    )
    held[...] = basis
    heldo[...] = prod[0:RANK] + prod[RANK : 2 * RANK] + prod[2 * RANK :]
    q = jnp.concatenate([held[mine, :], held[other, :]], axis=0)
    qo = jnp.concatenate([heldo[mine, :], heldo[other, :]], axis=0)
    lhs = jnp.concatenate(
        [jnp.concatenate(split3(qo), axis=0), jnp.concatenate(split3(q), axis=0)], axis=1
    )
    for c in range(0, WIDE, STEP):
        cols = slice(c, c + STEP)
        rhs = jnp.concatenate([a[:, cols] for a in (a0, a1, a2, a3, ef)], axis=0)
        p = jnp.dot(lhs, rhs, preferred_element_type=F32)
        r = p[0:RANK] + p[RANK : 2 * RANK] + p[2 * RANK :]
        for j in range(STEP // 128):
            chip = c // 128 + j
            keep[chip] = r[0:HALF, 128 * j : 128 * j + 128]
            send[chip] = r[HALF:, 128 * j : 128 * j + 128]


def spread_kernel(pieces, out):
    total = jnp.sum(pieces[...], axis=0) * (1.0 / REPLICAS)
    out[...] = jnp.broadcast_to(total[None], out.shape)


def finish_kernel(rown, roth, qt, og, a0, a1, a2, a3, ef, i0, i1, i2, i3, err, fac, igrad):
    t, core = lax.axis_index("t"), lax.axis_index("core")
    mine = pl.ds(pl.multiple_of(core * HALF, HALF), HALF)
    other = pl.ds(pl.multiple_of((1 - core) * HALF, HALF), HALF)
    for k, block in enumerate((i0, i1, i2, i3)):
        source = lax.rem(t - k + TENSOR, TENSOR)
        igrad[:, pl.ds(pl.multiple_of(source * PART, PART), PART)] = block[...]
    q = jnp.concatenate([qt[mine, :], qt[other, :]], axis=0)
    hi, mid = split2(q)
    hi, mid = hi.astype(F32), mid.astype(F32)
    ogp = turned(og, t).astype(F32)
    lhs = jnp.concatenate([ogp, -hi, -hi, -mid, -mid], axis=0).T.astype(BF16)
    for c in range(0, WIDE, STEP):
        cols = slice(c, c + STEP)
        ro = jnp.concatenate([rown[c // 128 + j] for j in range(STEP // 128)], axis=1)
        rt = jnp.concatenate([roth[c // 128 + j] for j in range(STEP // 128)], axis=1)
        fac[mine, cols] = ro.astype(BF16)
        fac[other, cols] = rt.astype(BF16)
        rhi, rmid = split2(jnp.concatenate([ro, rt], axis=0))
        rhs = jnp.concatenate([a[:, cols] for a in (a0, a1, a2, a3)] + [rhi, rmid, rhi, rmid], axis=0)
        total = jnp.dot(lhs, rhs, preferred_element_type=F32) + ef[:, cols].astype(F32)
        err[:, cols] = total.astype(BF16)


def input_kernel(w, og, r1, r2, r3, h0, h1, h2, h3, c0, c1, c2, c3, o0, o1, o2, o3, weights, feats):
    t, y, core = lax.axis_index("t"), lax.axis_index("y"), lax.axis_index("core")
    weights[0:128, :] = w[:, pl.ds(pl.multiple_of(t * PART, PART), PART)]
    feats[:, 0:128] = og[...]
    for k, r in enumerate((r1, r2, r3), 1):
        for m in range(8):
            feats[16 * m : 16 * m + 16, 128 * k : 128 * k + 128] = r[
                CUT : 2 * CUT, 128 * m : 128 * m + 128
            ]
        for j, (h, c) in enumerate(((h0, c0), (h1, c1), (h2, c2), (h3, c3))):
            first = 128 * k + 2 * CUT * lax.rem(y - j + 4, 4)
            here = pl.ds(pl.multiple_of(first + CUT * core, CUT), CUT)
            there = pl.ds(pl.multiple_of(first + CUT * (1 - core), CUT), CUT)
            weights[here, :] = h[CUT * (k - 1) : CUT * k, :]
            weights[there, :] = c[CUT * (k - 1) : CUT * k, :]
    for k, out in enumerate((o0, o1, o2, o3)):
        target = lax.rem(t + k, TENSOR)
        rows = feats[pl.ds(pl.multiple_of(target * OWN, OWN), OWN), :]
        out[...] = jnp.dot(rows, weights[...], preferred_element_type=F32).astype(BF16)


def moved(x, k, axis="t"):
    return lax.ppermute(x, axis, [(i, (i + k) % 4) for i in range(4)])


def swapped(x):
    return lax.ppermute(x, "core", [(0, 1), (1, 0)])


def exchanged(x, axes):
    return lax.all_to_all(x, axes, 0, 0, tiled=True)


def local(activations, out_grad, value_weight, error_feedback, warm_right):
    act, og, weight = activations[0], out_grad[0], value_weight[0]
    ef = error_feedback[0, 0]
    warm = warm_right[0, 0].T

    sends = call(pack_kernel, [((2 * CUT, PART), BF16)] * 3)(weight, og)
    got = [moved(x, k) for k, x in zip((1, 2, 3), sends)]
    act, got = lax.optimization_barrier((act, got))
    acts = [act] + [moved(act, k) for k in (1, 2, 3)]
    inner, fed, lines = call(
        early_kernel,
        [((RANK, OWN), F32), ((RANK, HEAD), F32), ((RANK, WIDE), BF16)],
        flops=0,
        moved=0,
    )(act, ef, warm)

    shares = [jnp.concatenate([g[:CUT] for g in got], axis=0)]
    shares += [moved(shares[0], j, "y") for j in (1, 2, 3)]
    outs = call(
        input_kernel,
        [((OWN, PART), BF16)] * 4,
        [pltpu.VMEM((512, PART), BF16), pltpu.VMEM((128, 512), BF16)],
        flops=0,
        moved=0,
    )(weight, og, *got, *shares, *[swapped(x) for x in shares])
    inputs = [outs[0]] + [moved(o, k) for k, o in zip((1, 2, 3), outs[1:])]

    half = ((HALF, HEAD), F32)
    left_keep, left_send = call(
        left_kernel, [half, half], [pltpu.VMEM((RANK, HEAD), F32)], flops=5 * 10**7, moved=10**6
    )(*acts[1:], og, lines, inner, fed)

    left_half = left_keep + swapped(left_send)
    left_half, inputs = lax.optimization_barrier((left_half, inputs))
    pieces = exchanged(jnp.broadcast_to(left_half[None], (N_CHIPS, HALF, HEAD)), CHIPS)
    left_own = jnp.sum(pieces, axis=0)
    left_other = swapped(left_own)

    block = ((N_CHIPS, HALF, 128), F32)
    basis, right_keep, right_send = call(
        basis_kernel,
        [((RANK, HEAD), F32), block, block],
        [pltpu.VMEM((RANK, HEAD), F32), pltpu.VMEM((RANK, HEAD), F32)],
        flops=10**8,
        moved=3 * 10**6,
    )(left_own, left_other, *acts, og, ef)

    pieces = exchanged(right_keep + swapped(right_send), CHIPS)
    (mean,) = call(spread_kernel, [block])(pieces)
    right_own = exchanged(mean, CHIPS)
    right_other = swapped(right_own)

    err, fac, igrad = call(
        finish_kernel,
        [((HEAD, WIDE), BF16), ((RANK, WIDE), BF16), ((OWN, WIDE), BF16)],
        flops=3 * 10**8,
        moved=5 * 10**6,
    )(right_own, right_other, basis, og, *acts, ef, *inputs)

    return (err[None, None], basis.T[None], fac.T[None, None], igrad[None])


def solution(mesh):
    parted = Mesh(
        mesh.devices.reshape(4, 2, 4, 2, 4), EVERY
    )
    return jax.shard_map(
        local,
        mesh=parted,
        in_specs=(
            P(None, EVERY, None),
            P(None, DP, "t"),
            P(None, "t", None),
            P(None, DP, "t", None),
            P(None, "t", None, None),
        ),
        out_specs=(
            P(None, DP, "t", None),
            P(None, "t", None),
            P(None, "t", None, None),
            P(None, EVERY, None),
        ),
        check_vma=False,
    )
```

```python
import jax
import jax.numpy as jnp
from jax import lax
from jax.experimental import pallas as pl
from jax.experimental.pallas import tpu as pltpu
from jax.sharding import Mesh
from jax.sharding import PartitionSpec as P

F32 = jnp.float32
BF16 = jnp.bfloat16
HIGH = lax.Precision.HIGHEST
CHIPS = ("x", "zl", "y")
DP = ("x", "zl", "y", "core")
EVERY = DP + ("t",)

TENSOR = 4
REPLICAS = 64
WIDE = 4096
HEAD = 128
RANK = 32
HALF = RANK // 2
OWN = 32
CUT = 16
PART = WIDE // TENSOR
N_CHIPS = REPLICAS // 2
STEP = 512
NT = (((1,), (1,)), ((), ()))


def split3(x):
    hi = x.astype(BF16)
    rest = x - hi.astype(F32)
    mid = rest.astype(BF16)
    low = (rest - mid.astype(F32)).astype(BF16)
    return (hi, mid, low)


def split2(x):
    hi = x.astype(BF16)
    return (hi, (x - hi.astype(F32)).astype(BF16))


def turned(ref, t):
    blocks = [ref[pl.ds(((t - k + TENSOR) % TENSOR) * OWN, OWN), :] for k in range(TENSOR)]
    return jnp.concatenate(blocks, axis=0)


def call(kernel, outs, scratch=(), flops=10**6, moved=10**6):
    vmem = pl.BlockSpec(memory_space=pltpu.VMEM)

    def run(*args):
        return pl.pallas_call(
            kernel,
            out_shape=[jax.ShapeDtypeStruct(s, d) for s, d in outs],
            in_specs=[vmem] * len(args),
            out_specs=[vmem] * len(outs),
            scratch_shapes=list(scratch),
            compiler_params=pltpu.CompilerParams(vmem_limit_bytes=40 * 2**20),
            cost_estimate=pl.CostEstimate(flops=flops, bytes_accessed=moved, transcendentals=0),
        )(*args)

    return run


def pack_kernel(w, og, *sends):
    t, y, core = lax.axis_index("t"), lax.axis_index("y"), lax.axis_index("core")
    rows = pl.ds(pl.multiple_of((2 * y + core) * CUT, CUT), CUT)
    for k, send in enumerate(sends, 1):
        target = lax.rem(t + k, TENSOR)
        send[0:CUT, :] = w[rows, pl.ds(pl.multiple_of(target * PART, PART), PART)]
        for m in range(8):
            send[CUT : 2 * CUT, 128 * m : 128 * m + 128] = og[16 * m : 16 * m + 16, :]


def early_kernel(a0, ef, warm, inner, fed, lines):
    lines[...] = warm[...]
    inner[...] = lax.dot_general(warm[...], a0[...], NT, preferred_element_type=F32)
    fed[...] = lax.dot_general(warm[...], ef[...], NT, preferred_element_type=F32)


def left_kernel(a1, a2, a3, og, lines, inner0, fed, keep, send, held):
    t, core = lax.axis_index("t"), lax.axis_index("core")
    ogp = turned(og, t)
    rest = [
        lax.dot_general(lines[...], a[...], NT, preferred_element_type=F32) for a in (a1, a2, a3)
    ]
    inner = jnp.concatenate([inner0[...]] + rest, axis=1)
    prod = jnp.dot(jnp.concatenate(split3(inner), axis=0), ogp, preferred_element_type=F32)
    held[...] = prod[0:RANK] + prod[RANK : 2 * RANK] + prod[2 * RANK :] + fed[...]
    keep[...] = held[pl.ds(pl.multiple_of(core * HALF, HALF), HALF), :]
    send[...] = held[pl.ds(pl.multiple_of((1 - core) * HALF, HALF), HALF), :]


def basis_kernel(lown, loth, a0, a1, a2, a3, og, ef, qt, keep, send, held, heldo):
    t, core = lax.axis_index("t"), lax.axis_index("core")
    mine = pl.ds(pl.multiple_of(core * HALF, HALF), HALF)
    other = pl.ds(pl.multiple_of((1 - core) * HALF, HALF), HALF)
    held[mine, :] = lown[...]
    held[other, :] = loth[...]
    left = held[...]
    gram = lax.dot_general(left, left, NT, precision=HIGH, preferred_element_type=F32)
    row = lax.broadcasted_iota(jnp.int32, (RANK, 1), 0)
    for k in range(RANK - 1):
        scale = 1.0 / gram[k : k + 1, k : k + 1]
        factor = jnp.where(row > k, gram[:, k : k + 1] * scale, 0.0)
        pivot_g, pivot_l = gram[k : k + 1, :], left[k : k + 1, :]
        gram = gram - factor * pivot_g
        left = left - factor * pivot_l
    eye = row == lax.broadcasted_iota(jnp.int32, (RANK, RANK), 1)
    diagonal = jnp.sum(jnp.where(eye, gram, 0.0), axis=1, keepdims=True)
    basis = left * (1.0 / jnp.sqrt(diagonal))
    qt[...] = basis
    ogp = turned(og, t)
    prod = lax.dot_general(
        jnp.concatenate(split3(basis), axis=0), ogp, NT, preferred_element_type=F32
    )
    held[...] = basis
    heldo[...] = prod[0:RANK] + prod[RANK : 2 * RANK] + prod[2 * RANK :]
    q = jnp.concatenate([held[mine, :], held[other, :]], axis=0)
    qo = jnp.concatenate([heldo[mine, :], heldo[other, :]], axis=0)
    lhs = jnp.concatenate(
        [jnp.concatenate(split3(qo), axis=0), jnp.concatenate(split3(q), axis=0)], axis=1
    )
    for c in range(0, WIDE, STEP):
        cols = slice(c, c + STEP)
        rhs = jnp.concatenate([a[:, cols] for a in (a0, a1, a2, a3, ef)], axis=0)
        p = jnp.dot(lhs, rhs, preferred_element_type=F32)
        r = p[0:RANK] + p[RANK : 2 * RANK] + p[2 * RANK :]
        for j in range(STEP // 128):
            chip = c // 128 + j
            keep[chip] = r[0:HALF, 128 * j : 128 * j + 128]
            send[chip] = r[HALF:, 128 * j : 128 * j + 128]


def spread_kernel(pieces, out):
    total = jnp.sum(pieces[...], axis=0) * (1.0 / REPLICAS)
    out[...] = jnp.broadcast_to(total[None], out.shape)


def finish_kernel(rown, roth, qt, og, a0, a1, a2, a3, ef, i0, i1, i2, i3, err, fac, igrad):
    t, core = lax.axis_index("t"), lax.axis_index("core")
    mine = pl.ds(pl.multiple_of(core * HALF, HALF), HALF)
    other = pl.ds(pl.multiple_of((1 - core) * HALF, HALF), HALF)
    for k, block in enumerate((i0, i1, i2, i3)):
        source = lax.rem(t - k + TENSOR, TENSOR)
        igrad[:, pl.ds(pl.multiple_of(source * PART, PART), PART)] = block[...]
    q = jnp.concatenate([qt[mine, :], qt[other, :]], axis=0)
    hi, mid = split2(q)
    hi, mid = hi.astype(F32), mid.astype(F32)
    ogp = turned(og, t).astype(F32)
    lhs = jnp.concatenate([ogp, -hi, -hi, -mid, -mid], axis=0).T.astype(BF16)
    for c in range(0, WIDE, STEP):
        cols = slice(c, c + STEP)
        ro = jnp.concatenate([rown[c // 128 + j] for j in range(STEP // 128)], axis=1)
        rt = jnp.concatenate([roth[c // 128 + j] for j in range(STEP // 128)], axis=1)
        fac[mine, cols] = ro.astype(BF16)
        fac[other, cols] = rt.astype(BF16)
        rhi, rmid = split2(jnp.concatenate([ro, rt], axis=0))
        rhs = jnp.concatenate([a[:, cols] for a in (a0, a1, a2, a3)] + [rhi, rmid, rhi, rmid], axis=0)
        total = jnp.dot(lhs, rhs, preferred_element_type=F32) + ef[:, cols].astype(F32)
        err[:, cols] = total.astype(BF16)


def input_kernel(w, og, r1, r2, r3, h0, h1, h2, h3, c0, c1, c2, c3, o0, o1, o2, o3, weights, feats):
    t, y, core = lax.axis_index("t"), lax.axis_index("y"), lax.axis_index("core")
    weights[0:128, :] = w[:, pl.ds(pl.multiple_of(t * PART, PART), PART)]
    feats[:, 0:128] = og[...]
    for k, r in enumerate((r1, r2, r3), 1):
        for m in range(8):
            feats[16 * m : 16 * m + 16, 128 * k : 128 * k + 128] = r[
                CUT : 2 * CUT, 128 * m : 128 * m + 128
            ]
        for j, (h, c) in enumerate(((h0, c0), (h1, c1), (h2, c2), (h3, c3))):
            first = 128 * k + 2 * CUT * lax.rem(y - j + 4, 4)
            here = pl.ds(pl.multiple_of(first + CUT * core, CUT), CUT)
            there = pl.ds(pl.multiple_of(first + CUT * (1 - core), CUT), CUT)
            weights[here, :] = h[CUT * (k - 1) : CUT * k, :]
            weights[there, :] = c[CUT * (k - 1) : CUT * k, :]
    for k, out in enumerate((o0, o1, o2, o3)):
        target = lax.rem(t + k, TENSOR)
        rows = feats[pl.ds(pl.multiple_of(target * OWN, OWN), OWN), :]
        out[...] = jnp.dot(rows, weights[...], preferred_element_type=F32).astype(BF16)


def moved(x, k, axis="t"):
    return lax.ppermute(x, axis, [(i, (i + k) % 4) for i in range(4)])


def swapped(x):
    return lax.ppermute(x, "core", [(0, 1), (1, 0)])


def exchanged(x, axes):
    return lax.all_to_all(x, axes, 0, 0, tiled=True)


def local(activations, out_grad, value_weight, error_feedback, warm_right):
    act, og, weight = activations[0], out_grad[0], value_weight[0]
    ef = error_feedback[0, 0]
    warm = warm_right[0, 0].T

    sends = call(pack_kernel, [((2 * CUT, PART), BF16)] * 3)(weight, og)
    got = [moved(x, k) for k, x in zip((1, 2, 3), sends)]
    acts = [act] + [moved(act, k) for k in (1, 2, 3)]
    inner, fed, lines = call(
        early_kernel,
        [((RANK, OWN), F32), ((RANK, HEAD), F32), ((RANK, WIDE), BF16)],
        flops=10**8,
        moved=3 * 10**6,
    )(act, ef, warm)

    half = ((HALF, HEAD), F32)
    left_keep, left_send = call(
        left_kernel, [half, half], [pltpu.VMEM((RANK, HEAD), F32)], flops=5 * 10**7, moved=10**6
    )(*acts[1:], og, lines, inner, fed)

    left_half = left_keep + swapped(left_send)
    left_half, got = lax.optimization_barrier((left_half, got))
    shares = [jnp.concatenate([g[:CUT] for g in got], axis=0)]
    shares += [moved(shares[0], j, "y") for j in (1, 2, 3)]
    traded = [swapped(x) for x in shares]
    pieces = exchanged(jnp.broadcast_to(left_half[None], (N_CHIPS, HALF, HEAD)), CHIPS)
    left_own = jnp.sum(pieces, axis=0)
    left_other = swapped(left_own)

    block = ((N_CHIPS, HALF, 128), F32)
    basis, right_keep, right_send = call(
        basis_kernel,
        [((RANK, HEAD), F32), block, block],
        [pltpu.VMEM((RANK, HEAD), F32), pltpu.VMEM((RANK, HEAD), F32)],
        flops=10**8,
        moved=3 * 10**6,
    )(left_own, left_other, *acts, og, ef)

    right_send, shares, traded = lax.optimization_barrier((right_send, shares, traded))
    outs = call(
        input_kernel,
        [((OWN, PART), BF16)] * 4,
        [pltpu.VMEM((512, PART), BF16), pltpu.VMEM((128, 512), BF16)],
        flops=2 * 10**8,
        moved=2 * 10**6,
    )(weight, og, *got, *shares, *traded)
    pieces = exchanged(right_keep + swapped(right_send), CHIPS)
    pieces, outs = lax.optimization_barrier((pieces, outs))
    (mean,) = call(spread_kernel, [block])(pieces)
    inputs = [outs[0]] + [moved(o, k) for k, o in zip((1, 2, 3), outs[1:])]
    right_own = exchanged(mean, CHIPS)
    right_own, inputs = lax.optimization_barrier((right_own, inputs))
    right_other = swapped(right_own)

    err, fac, igrad = call(
        finish_kernel,
        [((HEAD, WIDE), BF16), ((RANK, WIDE), BF16), ((OWN, WIDE), BF16)],
        flops=3 * 10**8,
        moved=5 * 10**6,
    )(right_own, right_other, basis, og, *acts, ef, *inputs)

    return (err[None, None], basis.T[None], fac.T[None, None], igrad[None])


def solution(mesh):
    parted = Mesh(
        mesh.devices.reshape(4, 2, 4, 2, 4), EVERY
    )
    return jax.shard_map(
        local,
        mesh=parted,
        in_specs=(
            P(None, EVERY, None),
            P(None, DP, "t"),
            P(None, "t", None),
            P(None, DP, "t", None),
            P(None, "t", None, None),
        ),
        out_specs=(
            P(None, DP, "t", None),
            P(None, "t", None),
            P(None, "t", None, None),
            P(None, EVERY, None),
        ),
        check_vma=False,
    )
```

```python
import jax
import jax.numpy as jnp
from jax import lax
from jax.experimental import pallas as pl
from jax.experimental.pallas import tpu as pltpu
from jax.sharding import Mesh
from jax.sharding import PartitionSpec as P

F32 = jnp.float32
BF16 = jnp.bfloat16
HIGH = lax.Precision.HIGHEST
CHIPS = ("x", "zl", "y")
DP = ("x", "zl", "y", "core")
EVERY = DP + ("t",)

TENSOR = 4
REPLICAS = 64
WIDE = 4096
HEAD = 128
RANK = 32
HALF = RANK // 2
OWN = 32
CUT = 16
PART = WIDE // TENSOR
N_CHIPS = REPLICAS // 2
STEP = 512
NT = (((1,), (1,)), ((), ()))


def split3(x):
    hi = x.astype(BF16)
    rest = x - hi.astype(F32)
    mid = rest.astype(BF16)
    low = (rest - mid.astype(F32)).astype(BF16)
    return (hi, mid, low)


def split2(x):
    hi = x.astype(BF16)
    return (hi, (x - hi.astype(F32)).astype(BF16))


def turned(ref, t):
    blocks = [ref[pl.ds(((t - k + TENSOR) % TENSOR) * OWN, OWN), :] for k in range(TENSOR)]
    return jnp.concatenate(blocks, axis=0)


def call(kernel, outs, scratch=(), flops=10**6, moved=10**6, space=pltpu.VMEM, dest=pltpu.VMEM, room=8):

    def run(*args):
        return pl.pallas_call(
            kernel,
            out_shape=[jax.ShapeDtypeStruct(s, d) for s, d in outs],
            in_specs=[pl.BlockSpec(memory_space=space)] * len(args),
            out_specs=[pl.BlockSpec(memory_space=dest)] * len(outs),
            scratch_shapes=list(scratch),
            compiler_params=pltpu.CompilerParams(vmem_limit_bytes=room * 2**20),
            cost_estimate=pl.CostEstimate(flops=flops, bytes_accessed=moved, transcendentals=0),
        )(*args)

    return run


def fetched(pairs, sems):
    copies = [pltpu.make_async_copy(a, b, sems.at[i]) for i, (a, b) in enumerate(pairs)]
    for copy in copies:
        copy.start()
    for copy in copies:
        copy.wait()


def pack_kernel(w, og, s1, s2, s3, lines, feats, packed, sems):
    t, y, core = lax.axis_index("t"), lax.axis_index("y"), lax.axis_index("core")
    rows = pl.ds(pl.multiple_of((2 * y + core) * CUT, CUT), CUT)
    fetched([(w.at[rows, :], lines), (og, feats)], sems)
    for k in range(1, TENSOR):
        target = lax.rem(t + k, TENSOR)
        packed[k - 1, 0:CUT, :] = lines[:, pl.ds(pl.multiple_of(target * PART, PART), PART)]
        for m in range(8):
            packed[k - 1, CUT : 2 * CUT, 128 * m : 128 * m + 128] = feats[16 * m : 16 * m + 16, :]
    fetched([(packed.at[k], send) for k, send in enumerate((s1, s2, s3))], sems)


def early_kernel(a0, ef, warm, inner, fed, lines):
    lines[...] = warm[...]
    inner[...] = lax.dot_general(warm[...], a0[...], NT, preferred_element_type=F32)
    fed[...] = lax.dot_general(warm[...], ef[...], NT, preferred_element_type=F32)


def left_kernel(a1, a2, a3, og, lines, inner0, fed, keep, send, held):
    t, core = lax.axis_index("t"), lax.axis_index("core")
    ogp = turned(og, t)
    rest = [
        lax.dot_general(lines[...], a[...], NT, preferred_element_type=F32) for a in (a1, a2, a3)
    ]
    inner = jnp.concatenate([inner0[...]] + rest, axis=1)
    prod = jnp.dot(jnp.concatenate(split3(inner), axis=0), ogp, preferred_element_type=F32)
    held[...] = prod[0:RANK] + prod[RANK : 2 * RANK] + prod[2 * RANK :] + fed[...]
    keep[...] = held[pl.ds(pl.multiple_of(core * HALF, HALF), HALF), :]
    send[...] = held[pl.ds(pl.multiple_of((1 - core) * HALF, HALF), HALF), :]


def basis_kernel(lown, loth, a0, a1, a2, a3, og, ef, qt, keep, send, held, heldo):
    t, core = lax.axis_index("t"), lax.axis_index("core")
    mine = pl.ds(pl.multiple_of(core * HALF, HALF), HALF)
    other = pl.ds(pl.multiple_of((1 - core) * HALF, HALF), HALF)
    held[mine, :] = lown[...]
    held[other, :] = loth[...]
    left = held[...]
    gram = lax.dot_general(left, left, NT, precision=HIGH, preferred_element_type=F32)
    row = lax.broadcasted_iota(jnp.int32, (RANK, 1), 0)
    for k in range(RANK - 1):
        scale = 1.0 / gram[k : k + 1, k : k + 1]
        factor = jnp.where(row > k, gram[:, k : k + 1] * scale, 0.0)
        pivot_g, pivot_l = gram[k : k + 1, :], left[k : k + 1, :]
        gram = gram - factor * pivot_g
        left = left - factor * pivot_l
    eye = row == lax.broadcasted_iota(jnp.int32, (RANK, RANK), 1)
    diagonal = jnp.sum(jnp.where(eye, gram, 0.0), axis=1, keepdims=True)
    basis = left * (1.0 / jnp.sqrt(diagonal))
    qt[...] = basis
    ogp = turned(og, t)
    prod = lax.dot_general(
        jnp.concatenate(split3(basis), axis=0), ogp, NT, preferred_element_type=F32
    )
    held[...] = basis
    heldo[...] = prod[0:RANK] + prod[RANK : 2 * RANK] + prod[2 * RANK :]
    q = jnp.concatenate([held[mine, :], held[other, :]], axis=0)
    qo = jnp.concatenate([heldo[mine, :], heldo[other, :]], axis=0)
    lhs = jnp.concatenate(
        [jnp.concatenate(split3(qo), axis=0), jnp.concatenate(split3(q), axis=0)], axis=1
    )
    for c in range(0, WIDE, STEP):
        cols = slice(c, c + STEP)
        rhs = jnp.concatenate([a[:, cols] for a in (a0, a1, a2, a3, ef)], axis=0)
        p = jnp.dot(lhs, rhs, preferred_element_type=F32)
        r = p[0:RANK] + p[RANK : 2 * RANK] + p[2 * RANK :]
        for j in range(STEP // 128):
            chip = c // 128 + j
            keep[chip] = r[0:HALF, 128 * j : 128 * j + 128]
            send[chip] = r[HALF:, 128 * j : 128 * j + 128]


def spread_kernel(pieces, out):
    total = jnp.sum(pieces[...], axis=0) * (1.0 / REPLICAS)
    out[...] = jnp.broadcast_to(total[None], out.shape)


def finish_kernel(rown, roth, qt, og, a0, a1, a2, a3, ef, i0, i1, i2, i3, err, fac, igrad):
    t, core = lax.axis_index("t"), lax.axis_index("core")
    mine = pl.ds(pl.multiple_of(core * HALF, HALF), HALF)
    other = pl.ds(pl.multiple_of((1 - core) * HALF, HALF), HALF)
    for k, block in enumerate((i0, i1, i2, i3)):
        source = lax.rem(t - k + TENSOR, TENSOR)
        igrad[:, pl.ds(pl.multiple_of(source * PART, PART), PART)] = block[...]
    q = jnp.concatenate([qt[mine, :], qt[other, :]], axis=0)
    hi, mid = split2(q)
    hi, mid = hi.astype(F32), mid.astype(F32)
    ogp = turned(og, t).astype(F32)
    lhs = jnp.concatenate([ogp, -hi, -hi, -mid, -mid], axis=0).T.astype(BF16)
    for c in range(0, WIDE, STEP):
        cols = slice(c, c + STEP)
        ro = jnp.concatenate([rown[c // 128 + j] for j in range(STEP // 128)], axis=1)
        rt = jnp.concatenate([roth[c // 128 + j] for j in range(STEP // 128)], axis=1)
        fac[mine, cols] = ro.astype(BF16)
        fac[other, cols] = rt.astype(BF16)
        rhi, rmid = split2(jnp.concatenate([ro, rt], axis=0))
        rhs = jnp.concatenate([a[:, cols] for a in (a0, a1, a2, a3)] + [rhi, rmid, rhi, rmid], axis=0)
        total = jnp.dot(lhs, rhs, preferred_element_type=F32) + ef[:, cols].astype(F32)
        err[:, cols] = total.astype(BF16)


def input_kernel(w, og, r1, r2, r3, h0, h1, h2, h3, c0, c1, c2, c3, *rest):
    *outs, rv, hv, cv, weights, feats, total, sems = rest
    t, y, core = lax.axis_index("t"), lax.axis_index("y"), lax.axis_index("core")
    mine = w.at[:, pl.ds(pl.multiple_of(t * PART, PART), PART)]
    pairs = [(mine, weights.at[pl.ds(0, 128), :]), (og, feats.at[:, pl.ds(0, 128)])]
    pairs += [(r, rv.at[k]) for k, r in enumerate((r1, r2, r3))]
    pairs += [(h, hv.at[j]) for j, h in enumerate((h0, h1, h2, h3))]
    pairs += [(c, cv.at[j]) for j, c in enumerate((c0, c1, c2, c3))]
    fetched(pairs, sems)
    for k in range(1, TENSOR):
        for m in range(8):
            feats[16 * m : 16 * m + 16, 128 * k : 128 * k + 128] = rv[
                k - 1, CUT : 2 * CUT, 128 * m : 128 * m + 128
            ]
        for j in range(4):
            first = 128 * k + 2 * CUT * lax.rem(y - j + 4, 4)
            here = pl.ds(pl.multiple_of(first + CUT * core, CUT), CUT)
            there = pl.ds(pl.multiple_of(first + CUT * (1 - core), CUT), CUT)
            weights[here, :] = hv[j, CUT * (k - 1) : CUT * k, :]
            weights[there, :] = cv[j, CUT * (k - 1) : CUT * k, :]
    for k in range(TENSOR):
        target = lax.rem(t + k, TENSOR)
        rows = feats[pl.ds(pl.multiple_of(target * OWN, OWN), OWN), :]
        total[k] = jnp.dot(rows, weights[...], preferred_element_type=F32).astype(BF16)
    fetched([(total.at[k], out) for k, out in enumerate(outs)], sems)


def moved(x, k, axis="t"):
    return lax.ppermute(x, axis, [(i, (i + k) % 4) for i in range(4)])


def swapped(x):
    return lax.ppermute(x, "core", [(0, 1), (1, 0)])


def exchanged(x, axes):
    return lax.all_to_all(x, axes, 0, 0, tiled=True)


def local(activations, out_grad, value_weight, error_feedback, warm_right):
    act, og, weight = activations[0], out_grad[0], value_weight[0]
    ef = error_feedback[0, 0]
    warm = warm_right[0, 0].T

    sends = call(
        pack_kernel,
        [((2 * CUT, PART), BF16)] * 3,
        [
            pltpu.VMEM((CUT, WIDE), BF16),
            pltpu.VMEM((128, HEAD), BF16),
            pltpu.VMEM((3, 2 * CUT, PART), BF16),
            pltpu.SemaphoreType.DMA((3,)),
        ],
        space=pltpu.MemorySpace.HBM,
        dest=pltpu.MemorySpace.HBM,
        room=60,
    )(weight, og)
    got = [moved(x, k) for k, x in zip((1, 2, 3), sends)]
    acts = [act] + [moved(act, k) for k in (1, 2, 3)]
    shares = [jnp.concatenate([g[:CUT] for g in got], axis=0)]
    shares += [moved(shares[0], j, "y") for j in (1, 2, 3)]
    traded = [swapped(x) for x in shares]
    inner, fed, lines = call(
        early_kernel,
        [((RANK, OWN), F32), ((RANK, HEAD), F32), ((RANK, WIDE), BF16)],
        flops=0,
        moved=0,
    )(act, ef, warm)

    half = ((HALF, HEAD), F32)
    left_keep, left_send = call(
        left_kernel, [half, half], [pltpu.VMEM((RANK, HEAD), F32)], flops=5 * 10**7, moved=10**6
    )(*acts[1:], og, lines, inner, fed)
    left_send, traded, shares = lax.optimization_barrier((left_send, traded, shares))

    left_half = left_keep + swapped(left_send)
    pieces = exchanged(jnp.broadcast_to(left_half[None], (N_CHIPS, HALF, HEAD)), CHIPS)
    outs = call(
        input_kernel,
        [((OWN, PART), BF16)] * 4,
        [
            pltpu.VMEM((3, 2 * CUT, PART), BF16),
            pltpu.VMEM((4, 3 * CUT, PART), BF16),
            pltpu.VMEM((4, 3 * CUT, PART), BF16),
            pltpu.VMEM((512, PART), BF16),
            pltpu.VMEM((128, 512), BF16),
            pltpu.VMEM((4, OWN, PART), BF16),
            pltpu.SemaphoreType.DMA((13,)),
        ],
        flops=2 * 10**8,
        moved=2 * 10**6,
        space=pltpu.MemorySpace.HBM,
        dest=pltpu.MemorySpace.HBM,
        room=60,
    )(weight, og, *got, *shares, *traded)
    inputs = [outs[0]] + [moved(o, k) for k, o in zip((1, 2, 3), outs[1:])]
    pieces, outs = lax.optimization_barrier((pieces, outs))
    left_own = jnp.sum(pieces, axis=0)
    left_other = swapped(left_own)

    block = ((N_CHIPS, HALF, 128), F32)
    basis, right_keep, right_send = call(
        basis_kernel,
        [((RANK, HEAD), F32), block, block],
        [pltpu.VMEM((RANK, HEAD), F32), pltpu.VMEM((RANK, HEAD), F32)],
        flops=10**8,
        moved=3 * 10**6,
    )(left_own, left_other, *acts, og, ef)

    pieces = exchanged(right_keep + swapped(right_send), CHIPS)
    pieces, inputs[1] = lax.optimization_barrier((pieces, inputs[1]))
    (mean,) = call(spread_kernel, [block])(pieces)
    right_own = exchanged(mean, CHIPS)
    right_own, inputs = lax.optimization_barrier((right_own, inputs))
    right_other = swapped(right_own)

    err, fac, igrad = call(
        finish_kernel,
        [((HEAD, WIDE), BF16), ((RANK, WIDE), BF16), ((OWN, WIDE), BF16)],
        flops=3 * 10**8,
        moved=5 * 10**6,
    )(right_own, right_other, basis, og, *acts, ef, *inputs)

    return (err[None, None], basis.T[None], fac.T[None, None], igrad[None])


def solution(mesh):
    parted = Mesh(
        mesh.devices.reshape(4, 2, 4, 2, 4), EVERY
    )
    return jax.shard_map(
        local,
        mesh=parted,
        in_specs=(
            P(None, EVERY, None),
            P(None, DP, "t"),
            P(None, "t", None),
            P(None, DP, "t", None),
            P(None, "t", None, None),
        ),
        out_specs=(
            P(None, DP, "t", None),
            P(None, "t", None),
            P(None, "t", None, None),
            P(None, EVERY, None),
        ),
        check_vma=False,
    )
```

```python
import jax
import jax.numpy as jnp
from jax import lax
from jax.experimental import pallas as pl
from jax.experimental.pallas import tpu as pltpu
from jax.sharding import Mesh
from jax.sharding import PartitionSpec as P

F32 = jnp.float32
BF16 = jnp.bfloat16
HIGH = lax.Precision.HIGHEST
CHIPS = ("x", "zl", "y")
DP = ("x", "zl", "y", "core")
EVERY = DP + ("t",)

TENSOR = 4
REPLICAS = 64
WIDE = 4096
HEAD = 128
RANK = 32
HALF = RANK // 2
OWN = 32
CUT = 256
PLANE = 16
N_CHIPS = REPLICAS // 2
STEP = 512
NT = (((1,), (1,)), ((), ()))


def split3(x):
    hi = x.astype(BF16)
    rest = x - hi.astype(F32)
    mid = rest.astype(BF16)
    low = (rest - mid.astype(F32)).astype(BF16)
    return (hi, mid, low)


def split2(x):
    hi = x.astype(BF16)
    return (hi, (x - hi.astype(F32)).astype(BF16))


def turned(ref, t):
    blocks = [ref[pl.ds(((t - k + TENSOR) % TENSOR) * OWN, OWN), :] for k in range(TENSOR)]
    return jnp.concatenate(blocks, axis=0)


def call(kernel, outs, scratch=(), flops=10**6, moved=10**6, space=pltpu.VMEM, dest=pltpu.VMEM, room=8):

    def run(*args):
        return pl.pallas_call(
            kernel,
            out_shape=[jax.ShapeDtypeStruct(s, d) for s, d in outs],
            in_specs=[pl.BlockSpec(memory_space=space)] * len(args),
            out_specs=[pl.BlockSpec(memory_space=dest)] * len(outs),
            scratch_shapes=list(scratch),
            compiler_params=pltpu.CompilerParams(vmem_limit_bytes=room * 2**20),
            cost_estimate=pl.CostEstimate(flops=flops, bytes_accessed=moved, transcendentals=0),
        )(*args)

    return run


def fetched(pairs, sems):
    copies = [pltpu.make_async_copy(a, b, sems.at[i]) for i, (a, b) in enumerate(pairs)]
    for copy in copies:
        copy.start()
    for copy in copies:
        copy.wait()


def plane():
    return 4 * lax.axis_index("x") + lax.axis_index("y")


def pack_kernel(w, og, s1, s2, s3, lines, feats, packed, sems):
    t = lax.axis_index("t")
    cols = pl.ds(pl.multiple_of(plane() * CUT, CUT), CUT)
    fetched([(w.at[:, cols], lines), (og, feats)], sems)
    for k in range(1, TENSOR):
        first = OWN * lax.rem(t + k, TENSOR)
        packed[k - 1, 0:HEAD, :] = lines[...]
        for h in range(2):
            rows = pl.ds(pl.multiple_of(first + 16 * h, 16), 16)
            packed[k - 1, HEAD : HEAD + 16, 128 * h : 128 * h + 128] = feats[rows, :]
    fetched([(packed.at[k], send) for k, send in enumerate((s1, s2, s3))], sems)


def rows_kernel(og, r1, r2, r3, out, held):
    t = lax.axis_index("t")
    held[:, 0:128] = og[pl.ds(pl.multiple_of(OWN * t, OWN), OWN), :]
    for k, r in enumerate((r1, r2, r3), 1):
        for h in range(2):
            held[16 * h : 16 * h + 16, 128 * k : 128 * k + 128] = r[
                HEAD : HEAD + 16, 128 * h : 128 * h + 128
            ]
    for g in range(PLANE):
        out[g] = held[...]


def early_kernel(a0, ef, warm, inner, fed, lines):
    lines[...] = warm[...]
    inner[...] = lax.dot_general(warm[...], a0[...], NT, preferred_element_type=F32)
    fed[...] = lax.dot_general(warm[...], ef[...], NT, preferred_element_type=F32)


def left_kernel(a1, a2, a3, og, lines, inner0, fed, keep, send, held):
    t, core = lax.axis_index("t"), lax.axis_index("core")
    ogp = turned(og, t)
    rest = [
        lax.dot_general(lines[...], a[...], NT, preferred_element_type=F32) for a in (a1, a2, a3)
    ]
    inner = jnp.concatenate([inner0[...]] + rest, axis=1)
    prod = jnp.dot(jnp.concatenate(split3(inner), axis=0), ogp, preferred_element_type=F32)
    held[...] = prod[0:RANK] + prod[RANK : 2 * RANK] + prod[2 * RANK :] + fed[...]
    keep[...] = held[pl.ds(pl.multiple_of(core * HALF, HALF), HALF), :]
    send[...] = held[pl.ds(pl.multiple_of((1 - core) * HALF, HALF), HALF), :]


def basis_kernel(lown, loth, a0, a1, a2, a3, og, ef, qt, keep, send, held, heldo):
    t, core = lax.axis_index("t"), lax.axis_index("core")
    mine = pl.ds(pl.multiple_of(core * HALF, HALF), HALF)
    other = pl.ds(pl.multiple_of((1 - core) * HALF, HALF), HALF)
    held[mine, :] = lown[...]
    held[other, :] = loth[...]
    left = held[...]
    gram = lax.dot_general(left, left, NT, precision=HIGH, preferred_element_type=F32)
    row = lax.broadcasted_iota(jnp.int32, (RANK, 1), 0)
    for k in range(RANK - 1):
        scale = 1.0 / gram[k : k + 1, k : k + 1]
        factor = jnp.where(row > k, gram[:, k : k + 1] * scale, 0.0)
        pivot_g, pivot_l = gram[k : k + 1, :], left[k : k + 1, :]
        gram = gram - factor * pivot_g
        left = left - factor * pivot_l
    eye = row == lax.broadcasted_iota(jnp.int32, (RANK, RANK), 1)
    diagonal = jnp.sum(jnp.where(eye, gram, 0.0), axis=1, keepdims=True)
    basis = left * (1.0 / jnp.sqrt(diagonal))
    qt[...] = basis
    ogp = turned(og, t)
    prod = lax.dot_general(
        jnp.concatenate(split3(basis), axis=0), ogp, NT, preferred_element_type=F32
    )
    held[...] = basis
    heldo[...] = prod[0:RANK] + prod[RANK : 2 * RANK] + prod[2 * RANK :]
    q = jnp.concatenate([held[mine, :], held[other, :]], axis=0)
    qo = jnp.concatenate([heldo[mine, :], heldo[other, :]], axis=0)
    lhs = jnp.concatenate(
        [jnp.concatenate(split3(qo), axis=0), jnp.concatenate(split3(q), axis=0)], axis=1
    )
    for c in range(0, WIDE, STEP):
        cols = slice(c, c + STEP)
        rhs = jnp.concatenate([a[:, cols] for a in (a0, a1, a2, a3, ef)], axis=0)
        p = jnp.dot(lhs, rhs, preferred_element_type=F32)
        r = p[0:RANK] + p[RANK : 2 * RANK] + p[2 * RANK :]
        for j in range(STEP // 128):
            chip = c // 128 + j
            keep[chip] = r[0:HALF, 128 * j : 128 * j + 128]
            send[chip] = r[HALF:, 128 * j : 128 * j + 128]


def spread_kernel(pieces, inputs, out):
    hi, mid = split2(jnp.sum(pieces[...], axis=0) * (1.0 / REPLICAS))
    for chip in range(N_CHIPS):
        g = chip // 8 * 4 + chip % 4
        out[chip, 0:16, :] = hi
        out[chip, 16:32, :] = mid
        out[chip, 32:64, :] = inputs[g, :, 0:128]
        out[chip, 64:96, :] = inputs[g, :, 128:256]


def finish_kernel(mixed, roth, qt, og, a0, a1, a2, a3, ef, err, fac, igrad):
    t, core = lax.axis_index("t"), lax.axis_index("core")
    zl = lax.axis_index("zl")
    mine = pl.ds(pl.multiple_of(core * HALF, HALF), HALF)
    other = pl.ds(pl.multiple_of((1 - core) * HALF, HALF), HALF)
    for g in range(PLANE):
        chip = g // 4 * 8 + 4 * zl + g % 4
        igrad[:, CUT * g : CUT * g + 128] = mixed[chip, 32:64, :]
        igrad[:, CUT * g + 128 : CUT * g + 256] = mixed[chip, 64:96, :]
    q = jnp.concatenate([qt[mine, :], qt[other, :]], axis=0)
    hi, mid = split2(q)
    hi, mid = hi.astype(F32), mid.astype(F32)
    ogp = turned(og, t).astype(F32)
    lhs = jnp.concatenate([ogp, -hi, -hi, -mid, -mid], axis=0).T.astype(BF16)
    for c in range(0, WIDE, STEP):
        cols = slice(c, c + STEP)
        chips = range(c // 128, (c + STEP) // 128)
        own = jnp.concatenate([mixed[j, 0:32, :] for j in chips], axis=1)
        oth = jnp.concatenate([roth[j] for j in chips], axis=1)
        fac[mine, cols] = own[0:16]
        fac[other, cols] = oth[0:16]
        high = jnp.concatenate([own[0:16], oth[0:16]], axis=0)
        low = jnp.concatenate([own[16:32], oth[16:32]], axis=0)
        rhs = jnp.concatenate(
            [a[:, cols] for a in (a0, a1, a2, a3)] + [high, low, high, low], axis=0
        )
        total = jnp.dot(lhs, rhs, preferred_element_type=F32) + ef[:, cols].astype(F32)
        err[:, cols] = total.astype(BF16)


def input_kernel(w, feats, r1, r2, r3, out, fv, weights, total, sems):
    cols = pl.ds(pl.multiple_of(plane() * CUT, CUT), CUT)
    pairs = [(w.at[:, cols], weights.at[pl.ds(0, HEAD), :]), (feats, fv)]
    pairs += [
        (r.at[pl.ds(0, HEAD), :], weights.at[pl.ds(HEAD * k, HEAD), :])
        for k, r in enumerate((r1, r2, r3), 1)
    ]
    fetched(pairs, sems)
    for g in range(0, PLANE, 4):
        rows = jnp.concatenate([fv[g + i] for i in range(4)], axis=0)
        part = jnp.dot(rows, weights[...], preferred_element_type=F32).astype(BF16)
        for i in range(4):
            total[g + i] = part[OWN * i : OWN * i + OWN]
    fetched([(total, out)], sems)


def moved(x, k, axis="t"):
    return lax.ppermute(x, axis, [(i, (i + k) % 4) for i in range(4)])


def swapped(x):
    return lax.ppermute(x, "core", [(0, 1), (1, 0)])


def exchanged(x, axes):
    return lax.all_to_all(x, axes, 0, 0, tiled=True)


def local(activations, out_grad, value_weight, error_feedback, warm_right):
    act, og, weight = activations[0], out_grad[0], value_weight[0]
    ef = error_feedback[0, 0]
    warm = warm_right[0, 0].T

    sends = call(
        pack_kernel,
        [((HEAD + 16, CUT), BF16)] * 3,
        [
            pltpu.VMEM((HEAD, CUT), BF16),
            pltpu.VMEM((128, HEAD), BF16),
            pltpu.VMEM((3, HEAD + 16, CUT), BF16),
            pltpu.SemaphoreType.DMA((3,)),
        ],
        space=pltpu.MemorySpace.HBM,
        dest=pltpu.MemorySpace.HBM,
        room=60,
    )(weight, og)
    got = [moved(x, k) for k, x in zip((1, 2, 3), sends)]
    acts = [act] + [moved(act, k) for k in (1, 2, 3)]
    (rows,) = call(rows_kernel, [((PLANE, OWN, 512), BF16)], [pltpu.VMEM((OWN, 512), BF16)])(og, *got)
    feats = exchanged(rows, ("x", "y"))
    inner, fed, lines = call(
        early_kernel,
        [((RANK, OWN), F32), ((RANK, HEAD), F32), ((RANK, WIDE), BF16)],
        flops=10**10,
        moved=10**8,
    )(act, ef, warm)

    half = ((HALF, HEAD), F32)
    left_keep, left_send = call(
        left_kernel, [half, half], [pltpu.VMEM((RANK, HEAD), F32)], flops=5 * 10**7, moved=10**6
    )(*acts[1:], og, lines, inner, fed)
    left_send, feats = lax.optimization_barrier((left_send, feats))

    left_half = left_keep + swapped(left_send)
    pieces = exchanged(jnp.broadcast_to(left_half[None], (N_CHIPS, HALF, HEAD)), CHIPS)
    (inputs,) = call(
        input_kernel,
        [((PLANE, OWN, CUT), BF16)],
        [
            pltpu.VMEM((PLANE, OWN, 512), BF16),
            pltpu.VMEM((512, CUT), BF16),
            pltpu.VMEM((PLANE, OWN, CUT), BF16),
            pltpu.SemaphoreType.DMA((5,)),
        ],
        flops=2 * 10**8,
        moved=2 * 10**6,
        space=pltpu.MemorySpace.HBM,
        dest=pltpu.MemorySpace.HBM,
        room=60,
    )(weight, feats, *got)
    pieces, inputs = lax.optimization_barrier((pieces, inputs))
    left_own = jnp.sum(pieces, axis=0)
    left_other = swapped(left_own)

    block = ((N_CHIPS, HALF, 128), F32)
    basis, right_keep, right_send = call(
        basis_kernel,
        [((RANK, HEAD), F32), block, block],
        [pltpu.VMEM((RANK, HEAD), F32), pltpu.VMEM((RANK, HEAD), F32)],
        flops=10**8,
        moved=3 * 10**6,
    )(left_own, left_other, *acts, og, ef)

    pieces = exchanged(right_keep + swapped(right_send), CHIPS)
    (mixed,) = call(spread_kernel, [((N_CHIPS, 96, 128), BF16)])(pieces, inputs)
    mixed = exchanged(mixed, CHIPS)
    right_other = swapped(mixed[:, 0:32])

    err, fac, igrad = call(
        finish_kernel,
        [((HEAD, WIDE), BF16), ((RANK, WIDE), BF16), ((OWN, WIDE), BF16)],
        flops=3 * 10**8,
        moved=5 * 10**6,
    )(mixed, right_other, basis, og, *acts, ef)

    return (err[None, None], basis.T[None], fac.T[None, None], igrad[None])


def solution(mesh):
    parted = Mesh(
        mesh.devices.reshape(4, 2, 4, 2, 4), EVERY
    )
    return jax.shard_map(
        local,
        mesh=parted,
        in_specs=(
            P(None, EVERY, None),
            P(None, DP, "t"),
            P(None, "t", None),
            P(None, DP, "t", None),
            P(None, "t", None, None),
        ),
        out_specs=(
            P(None, DP, "t", None),
            P(None, "t", None),
            P(None, "t", None, None),
            P(None, EVERY, None),
        ),
        check_vma=False,
    )
```

```python
import jax
import jax.numpy as jnp
from jax import lax
from jax.experimental import pallas as pl
from jax.experimental.pallas import tpu as pltpu
from jax.sharding import Mesh
from jax.sharding import PartitionSpec as P

F32 = jnp.float32
BF16 = jnp.bfloat16
HIGH = lax.Precision.HIGHEST
CHIPS = ("x", "zl", "y")
DP = ("x", "zl", "y", "core")
EVERY = DP + ("t",)

TENSOR = 4
REPLICAS = 64
WIDE = 4096
HEAD = 128
RANK = 32
HALF = RANK // 2
OWN = 32
CUT = 256
PLANE = 16
N_CHIPS = REPLICAS // 2
STEP = 512
NT = (((1,), (1,)), ((), ()))


def split3(x):
    hi = x.astype(BF16)
    rest = x - hi.astype(F32)
    mid = rest.astype(BF16)
    low = (rest - mid.astype(F32)).astype(BF16)
    return (hi, mid, low)


def split2(x):
    hi = x.astype(BF16)
    return (hi, (x - hi.astype(F32)).astype(BF16))


def turned(ref, t):
    blocks = [ref[pl.ds(((t - k + TENSOR) % TENSOR) * OWN, OWN), :] for k in range(TENSOR)]
    return jnp.concatenate(blocks, axis=0)


def call(kernel, outs, scratch=(), flops=10**6, moved=10**6, space=pltpu.VMEM, dest=pltpu.VMEM, room=8):

    def run(*args):
        return pl.pallas_call(
            kernel,
            out_shape=[jax.ShapeDtypeStruct(s, d) for s, d in outs],
            in_specs=[pl.BlockSpec(memory_space=space)] * len(args),
            out_specs=[pl.BlockSpec(memory_space=dest)] * len(outs),
            scratch_shapes=list(scratch),
            compiler_params=pltpu.CompilerParams(vmem_limit_bytes=room * 2**20),
            cost_estimate=pl.CostEstimate(flops=flops, bytes_accessed=moved, transcendentals=0),
        )(*args)

    return run


def fetched(pairs, sems):
    copies = [pltpu.make_async_copy(a, b, sems.at[i]) for i, (a, b) in enumerate(pairs)]
    for copy in copies:
        copy.start()
    for copy in copies:
        copy.wait()


def plane():
    return 4 * lax.axis_index("x") + lax.axis_index("y")


def pack_kernel(w, og, s1, s2, s3, feats, sems):
    t, core = lax.axis_index("t"), lax.axis_index("core")
    cols = pl.ds(pl.multiple_of(plane() * CUT, CUT), CUT)
    part = w.at[pl.ds(pl.multiple_of(core * 64, 64), 64), cols]
    sends = (s1, s2, s3)
    fetched([(part, s.at[pl.ds(0, 64), :]) for s in sends] + [(og, feats)], sems)
    for k, send in enumerate(sends, 1):
        first = OWN * lax.rem(t + k, TENSOR)
        for h in range(2):
            rows = pl.ds(pl.multiple_of(first + 16 * h, 16), 16)
            send[64:80, 128 * h : 128 * h + 128] = feats[rows, :]


def rows_kernel(og, r1, r2, r3, out, held):
    t = lax.axis_index("t")
    held[:, 0:128] = og[pl.ds(pl.multiple_of(OWN * t, OWN), OWN), :]
    for k, r in enumerate((r1, r2, r3), 1):
        for h in range(2):
            held[16 * h : 16 * h + 16, 128 * k : 128 * k + 128] = r[
                64:80, 128 * h : 128 * h + 128
            ]
    for g in range(PLANE):
        out[g] = held[...]


def early_kernel(a0, ef, warm, inner, fed, lines):
    lines[...] = warm[...]
    inner[...] = lax.dot_general(warm[...], a0[...], NT, preferred_element_type=F32)
    fed[...] = lax.dot_general(warm[...], ef[...], NT, preferred_element_type=F32)


def left_kernel(a1, a2, a3, og, lines, inner0, fed, keep, send, held):
    t, core = lax.axis_index("t"), lax.axis_index("core")
    ogp = turned(og, t)
    rest = [
        lax.dot_general(lines[...], a[...], NT, preferred_element_type=F32) for a in (a1, a2, a3)
    ]
    inner = jnp.concatenate([inner0[...]] + rest, axis=1)
    prod = jnp.dot(jnp.concatenate(split3(inner), axis=0), ogp, preferred_element_type=F32)
    held[...] = prod[0:RANK] + prod[RANK : 2 * RANK] + prod[2 * RANK :] + fed[...]
    keep[...] = held[pl.ds(pl.multiple_of(core * HALF, HALF), HALF), :]
    send[...] = held[pl.ds(pl.multiple_of((1 - core) * HALF, HALF), HALF), :]


def basis_kernel(lown, loth, a0, a1, a2, a3, og, ef, qt, keep, send, held, heldo):
    t, core = lax.axis_index("t"), lax.axis_index("core")
    mine = pl.ds(pl.multiple_of(core * HALF, HALF), HALF)
    other = pl.ds(pl.multiple_of((1 - core) * HALF, HALF), HALF)
    held[mine, :] = lown[...]
    held[other, :] = loth[...]
    left = held[...]
    gram = lax.dot_general(left, left, NT, precision=HIGH, preferred_element_type=F32)
    row = lax.broadcasted_iota(jnp.int32, (RANK, 1), 0)
    for k in range(RANK - 1):
        scale = 1.0 / gram[k : k + 1, k : k + 1]
        factor = jnp.where(row > k, gram[:, k : k + 1] * scale, 0.0)
        pivot_g, pivot_l = gram[k : k + 1, :], left[k : k + 1, :]
        gram = gram - factor * pivot_g
        left = left - factor * pivot_l
    eye = row == lax.broadcasted_iota(jnp.int32, (RANK, RANK), 1)
    diagonal = jnp.sum(jnp.where(eye, gram, 0.0), axis=1, keepdims=True)
    basis = left * (1.0 / jnp.sqrt(diagonal))
    qt[...] = basis
    ogp = turned(og, t)
    prod = lax.dot_general(
        jnp.concatenate(split3(basis), axis=0), ogp, NT, preferred_element_type=F32
    )
    held[...] = basis
    heldo[...] = prod[0:RANK] + prod[RANK : 2 * RANK] + prod[2 * RANK :]
    q = jnp.concatenate([held[mine, :], held[other, :]], axis=0)
    qo = jnp.concatenate([heldo[mine, :], heldo[other, :]], axis=0)
    lhs = jnp.concatenate(
        [jnp.concatenate(split3(qo), axis=0), jnp.concatenate(split3(q), axis=0)], axis=1
    )
    for c in range(0, WIDE, STEP):
        cols = slice(c, c + STEP)
        rhs = jnp.concatenate([a[:, cols] for a in (a0, a1, a2, a3, ef)], axis=0)
        p = jnp.dot(lhs, rhs, preferred_element_type=F32)
        r = p[0:RANK] + p[RANK : 2 * RANK] + p[2 * RANK :]
        for j in range(STEP // 128):
            chip = c // 128 + j
            keep[chip] = r[0:HALF, 128 * j : 128 * j + 128]
            send[chip] = r[HALF:, 128 * j : 128 * j + 128]


def spread_kernel(pieces, inputs, out):
    hi, mid = split2(jnp.sum(pieces[...], axis=0) * (1.0 / REPLICAS))
    for chip in range(N_CHIPS):
        g = chip // 8 * 4 + chip % 4
        out[chip, 0:16, :] = hi
        out[chip, 16:32, :] = mid
        out[chip, 32:64, :] = inputs[g, :, 0:128]
        out[chip, 64:96, :] = inputs[g, :, 128:256]


def finish_kernel(mixed, roth, qt, og, a0, a1, a2, a3, ef, err, fac, igrad):
    t, core = lax.axis_index("t"), lax.axis_index("core")
    zl = lax.axis_index("zl")
    mine = pl.ds(pl.multiple_of(core * HALF, HALF), HALF)
    other = pl.ds(pl.multiple_of((1 - core) * HALF, HALF), HALF)
    for g in range(PLANE):
        chip = g // 4 * 8 + 4 * zl + g % 4
        igrad[:, CUT * g : CUT * g + 128] = mixed[chip, 32:64, :]
        igrad[:, CUT * g + 128 : CUT * g + 256] = mixed[chip, 64:96, :]
    q = jnp.concatenate([qt[mine, :], qt[other, :]], axis=0)
    hi, mid = split2(q)
    hi, mid = hi.astype(F32), mid.astype(F32)
    ogp = turned(og, t).astype(F32)
    lhs = jnp.concatenate([ogp, -hi, -hi, -mid, -mid], axis=0).T.astype(BF16)
    for c in range(0, WIDE, STEP):
        cols = slice(c, c + STEP)
        chips = range(c // 128, (c + STEP) // 128)
        own = jnp.concatenate([mixed[j, 0:32, :] for j in chips], axis=1)
        oth = jnp.concatenate([roth[j] for j in chips], axis=1)
        fac[mine, cols] = own[0:16]
        fac[other, cols] = oth[0:16]
        high = jnp.concatenate([own[0:16], oth[0:16]], axis=0)
        low = jnp.concatenate([own[16:32], oth[16:32]], axis=0)
        rhs = jnp.concatenate(
            [a[:, cols] for a in (a0, a1, a2, a3)] + [high, low, high, low], axis=0
        )
        total = jnp.dot(lhs, rhs, preferred_element_type=F32) + ef[:, cols].astype(F32)
        err[:, cols] = total.astype(BF16)


def input_kernel(w, feats, r1, r2, r3, c1, c2, c3, out, fv, weights, total, sems):
    core = lax.axis_index("core")
    cols = pl.ds(pl.multiple_of(plane() * CUT, CUT), CUT)
    pairs = [(w.at[:, cols], weights.at[pl.ds(0, HEAD), :]), (feats, fv)]
    for k, (r, c) in enumerate(((r1, c1), (r2, c2), (r3, c3)), 1):
        for source, side in ((r, core), (c, 1 - core)):
            rows = pl.ds(pl.multiple_of(HEAD * k + 64 * side, 64), 64)
            pairs.append((source.at[pl.ds(0, 64), :], weights.at[rows, :]))
    fetched(pairs, sems)
    for g in range(0, PLANE, 4):
        rows = jnp.concatenate([fv[g + i] for i in range(4)], axis=0)
        part = jnp.dot(rows, weights[...], preferred_element_type=F32).astype(BF16)
        for i in range(4):
            total[g + i] = part[OWN * i : OWN * i + OWN]
    fetched([(total, out)], sems)


def moved(x, k, axis="t"):
    return lax.ppermute(x, axis, [(i, (i + k) % 4) for i in range(4)])


def swapped(x):
    return lax.ppermute(x, "core", [(0, 1), (1, 0)])


def exchanged(x, axes):
    return lax.all_to_all(x, axes, 0, 0, tiled=True)


def local(activations, out_grad, value_weight, error_feedback, warm_right):
    act, og, weight = activations[0], out_grad[0], value_weight[0]
    ef = error_feedback[0, 0]
    warm = warm_right[0, 0].T

    sends = call(
        pack_kernel,
        [((80, CUT), BF16)] * 3,
        [pltpu.VMEM((128, HEAD), BF16), pltpu.SemaphoreType.DMA((4,))],
        space=pltpu.MemorySpace.HBM,
        room=60,
    )(weight, og)
    got = [moved(x, k) for k, x in zip((1, 2, 3), sends)]
    acts = [act] + [moved(act, k) for k in (1, 2, 3)]
    (rows,) = call(rows_kernel, [((PLANE, OWN, 512), BF16)], [pltpu.VMEM((OWN, 512), BF16)])(og, *got)
    feats = exchanged(rows, ("x", "y"))
    traded = [swapped(g) for g in got]
    inner, fed, lines = call(
        early_kernel,
        [((RANK, OWN), F32), ((RANK, HEAD), F32), ((RANK, WIDE), BF16)],
        flops=10**10,
        moved=10**8,
    )(act, ef, warm)

    half = ((HALF, HEAD), F32)
    left_keep, left_send = call(
        left_kernel, [half, half], [pltpu.VMEM((RANK, HEAD), F32)], flops=5 * 10**7, moved=10**6
    )(*acts[1:], og, lines, inner, fed)
    left_send, feats, traded = lax.optimization_barrier((left_send, feats, traded))

    left_half = left_keep + swapped(left_send)
    pieces = exchanged(jnp.broadcast_to(left_half[None], (N_CHIPS, HALF, HEAD)), CHIPS)
    (inputs,) = call(
        input_kernel,
        [((PLANE, OWN, CUT), BF16)],
        [
            pltpu.VMEM((PLANE, OWN, 512), BF16),
            pltpu.VMEM((512, CUT), BF16),
            pltpu.VMEM((PLANE, OWN, CUT), BF16),
            pltpu.SemaphoreType.DMA((8,)),
        ],
        flops=2 * 10**8,
        moved=2 * 10**6,
        space=pltpu.MemorySpace.HBM,
        dest=pltpu.MemorySpace.HBM,
        room=60,
    )(weight, feats, *got, *traded)
    pieces, inputs = lax.optimization_barrier((pieces, inputs))
    left_own = jnp.sum(pieces, axis=0)
    left_other = swapped(left_own)

    block = ((N_CHIPS, HALF, 128), F32)
    basis, right_keep, right_send = call(
        basis_kernel,
        [((RANK, HEAD), F32), block, block],
        [pltpu.VMEM((RANK, HEAD), F32), pltpu.VMEM((RANK, HEAD), F32)],
        flops=10**8,
        moved=3 * 10**6,
    )(left_own, left_other, *acts, og, ef)

    pieces = exchanged(right_keep + swapped(right_send), CHIPS)
    (mixed,) = call(spread_kernel, [((N_CHIPS, 96, 128), BF16)])(pieces, inputs)
    mixed = exchanged(mixed, CHIPS)
    right_other = swapped(mixed[:, 0:32])

    err, fac, igrad = call(
        finish_kernel,
        [((HEAD, WIDE), BF16), ((RANK, WIDE), BF16), ((OWN, WIDE), BF16)],
        flops=3 * 10**8,
        moved=5 * 10**6,
    )(mixed, right_other, basis, og, *acts, ef)

    return (err[None, None], basis.T[None], fac.T[None, None], igrad[None])


def solution(mesh):
    parted = Mesh(
        mesh.devices.reshape(4, 2, 4, 2, 4), EVERY
    )
    return jax.shard_map(
        local,
        mesh=parted,
        in_specs=(
            P(None, EVERY, None),
            P(None, DP, "t"),
            P(None, "t", None),
            P(None, DP, "t", None),
            P(None, "t", None, None),
        ),
        out_specs=(
            P(None, DP, "t", None),
            P(None, "t", None),
            P(None, "t", None, None),
            P(None, EVERY, None),
        ),
        check_vma=False,
    )
```

```python
import jax
import jax.numpy as jnp
from jax import lax
from jax.experimental import pallas as pl
from jax.experimental.pallas import tpu as pltpu
from jax.sharding import Mesh
from jax.sharding import PartitionSpec as P

F32 = jnp.float32
BF16 = jnp.bfloat16
HIGH = lax.Precision.HIGHEST
CHIPS = ("x", "zl", "y")
DP = ("x", "zl", "y", "core")
EVERY = DP + ("t",)

TENSOR = 4
REPLICAS = 64
WIDE = 4096
HEAD = 128
RANK = 32
HALF = RANK // 2
OWN = 32
CUT = 256
PLANE = 16
N_CHIPS = REPLICAS // 2
STEP = 512
NT = (((1,), (1,)), ((), ()))


def split3(x):
    hi = x.astype(BF16)
    rest = x - hi.astype(F32)
    mid = rest.astype(BF16)
    low = (rest - mid.astype(F32)).astype(BF16)
    return (hi, mid, low)


def split2(x):
    hi = x.astype(BF16)
    return (hi, (x - hi.astype(F32)).astype(BF16))


def turned(ref, t):
    blocks = [ref[pl.ds(((t - k + TENSOR) % TENSOR) * OWN, OWN), :] for k in range(TENSOR)]
    return jnp.concatenate(blocks, axis=0)


def call(kernel, outs, scratch=(), flops=10**6, moved=10**6, space=pltpu.VMEM, dest=pltpu.VMEM, room=8):

    def run(*args):
        return pl.pallas_call(
            kernel,
            out_shape=[jax.ShapeDtypeStruct(s, d) for s, d in outs],
            in_specs=[pl.BlockSpec(memory_space=space)] * len(args),
            out_specs=[pl.BlockSpec(memory_space=dest)] * len(outs),
            scratch_shapes=list(scratch),
            compiler_params=pltpu.CompilerParams(vmem_limit_bytes=room * 2**20),
            cost_estimate=pl.CostEstimate(flops=flops, bytes_accessed=moved, transcendentals=0),
        )(*args)

    return run


def fetched(pairs, sems):
    copies = [pltpu.make_async_copy(a, b, sems.at[i]) for i, (a, b) in enumerate(pairs)]
    for copy in copies:
        copy.start()
    for copy in copies:
        copy.wait()


def plane():
    return 4 * lax.axis_index("x") + lax.axis_index("y")


def pack_kernel(w, og, s1, s2, s3, feats, sems):
    t = lax.axis_index("t")
    part = w.at[:, pl.ds(pl.multiple_of(plane() * CUT, CUT), CUT)]
    sends = (s1, s2, s3)
    fetched([(part, s.at[pl.ds(0, HEAD), :]) for s in sends] + [(og, feats)], sems)
    for k, send in enumerate(sends, 1):
        first = OWN * lax.rem(t + k, TENSOR)
        for h in range(2):
            rows = pl.ds(pl.multiple_of(first + 16 * h, 16), 16)
            send[HEAD : HEAD + 16, 128 * h : 128 * h + 128] = feats[rows, :]


def rows_kernel(og, r1, r2, r3, out, held):
    t = lax.axis_index("t")
    held[:, 0:128] = og[pl.ds(pl.multiple_of(OWN * t, OWN), OWN), :]
    for k, r in enumerate((r1, r2, r3), 1):
        for h in range(2):
            held[16 * h : 16 * h + 16, 128 * k : 128 * k + 128] = r[
                HEAD : HEAD + 16, 128 * h : 128 * h + 128
            ]
    for g in range(PLANE):
        out[g] = held[...]


def early_kernel(a0, ef, warm, inner, fed, lines):
    lines[...] = warm[...]
    inner[...] = lax.dot_general(warm[...], a0[...], NT, preferred_element_type=F32)
    fed[...] = lax.dot_general(warm[...], ef[...], NT, preferred_element_type=F32)


def left_kernel(a1, a2, a3, og, lines, inner0, fed, keep, send, held):
    t, core = lax.axis_index("t"), lax.axis_index("core")
    ogp = turned(og, t)
    rest = [
        lax.dot_general(lines[...], a[...], NT, preferred_element_type=F32) for a in (a1, a2, a3)
    ]
    inner = jnp.concatenate([inner0[...]] + rest, axis=1)
    prod = jnp.dot(jnp.concatenate(split3(inner), axis=0), ogp, preferred_element_type=F32)
    held[...] = prod[0:RANK] + prod[RANK : 2 * RANK] + prod[2 * RANK :] + fed[...]
    keep[...] = held[pl.ds(pl.multiple_of(core * HALF, HALF), HALF), :]
    send[...] = held[pl.ds(pl.multiple_of((1 - core) * HALF, HALF), HALF), :]


def basis_kernel(lown, loth, a0, a1, a2, a3, og, ef, qt, keep, send, held, heldo):
    t, core = lax.axis_index("t"), lax.axis_index("core")
    mine = pl.ds(pl.multiple_of(core * HALF, HALF), HALF)
    other = pl.ds(pl.multiple_of((1 - core) * HALF, HALF), HALF)
    held[mine, :] = lown[...]
    held[other, :] = loth[...]
    left = held[...]
    gram = lax.dot_general(left, left, NT, precision=HIGH, preferred_element_type=F32)
    row = lax.broadcasted_iota(jnp.int32, (RANK, 1), 0)
    for k in range(RANK - 1):
        scale = 1.0 / gram[k : k + 1, k : k + 1]
        factor = jnp.where(row > k, gram[:, k : k + 1] * scale, 0.0)
        pivot_g, pivot_l = gram[k : k + 1, :], left[k : k + 1, :]
        gram = gram - factor * pivot_g
        left = left - factor * pivot_l
    eye = row == lax.broadcasted_iota(jnp.int32, (RANK, RANK), 1)
    diagonal = jnp.sum(jnp.where(eye, gram, 0.0), axis=1, keepdims=True)
    basis = left * (1.0 / jnp.sqrt(diagonal))
    qt[...] = basis
    ogp = turned(og, t)
    prod = lax.dot_general(
        jnp.concatenate(split3(basis), axis=0), ogp, NT, preferred_element_type=F32
    )
    held[...] = basis
    heldo[...] = prod[0:RANK] + prod[RANK : 2 * RANK] + prod[2 * RANK :]
    q = jnp.concatenate([held[mine, :], held[other, :]], axis=0)
    qo = jnp.concatenate([heldo[mine, :], heldo[other, :]], axis=0)
    lhs = jnp.concatenate(
        [jnp.concatenate(split3(qo), axis=0), jnp.concatenate(split3(q), axis=0)], axis=1
    )
    for c in range(0, WIDE, STEP):
        cols = slice(c, c + STEP)
        rhs = jnp.concatenate([a[:, cols] for a in (a0, a1, a2, a3, ef)], axis=0)
        p = jnp.dot(lhs, rhs, preferred_element_type=F32)
        r = p[0:RANK] + p[RANK : 2 * RANK] + p[2 * RANK :]
        for j in range(STEP // 128):
            chip = c // 128 + j
            keep[chip] = r[0:HALF, 128 * j : 128 * j + 128]
            send[chip] = r[HALF:, 128 * j : 128 * j + 128]


def spread_kernel(pieces, inputs, out):
    hi, mid = split2(jnp.sum(pieces[...], axis=0) * (1.0 / REPLICAS))
    for chip in range(N_CHIPS):
        g = chip // 8 * 4 + chip % 4
        out[chip, 0:16, :] = hi
        out[chip, 16:32, :] = mid
        out[chip, 32:64, :] = inputs[g, :, 0:128]
        out[chip, 64:96, :] = inputs[g, :, 128:256]


def finish_kernel(mixed, roth, qt, og, a0, a1, a2, a3, ef, err, fac, igrad):
    t, core = lax.axis_index("t"), lax.axis_index("core")
    zl = lax.axis_index("zl")
    mine = pl.ds(pl.multiple_of(core * HALF, HALF), HALF)
    other = pl.ds(pl.multiple_of((1 - core) * HALF, HALF), HALF)
    for g in range(PLANE):
        chip = g // 4 * 8 + 4 * zl + g % 4
        igrad[:, CUT * g : CUT * g + 128] = mixed[chip, 32:64, :]
        igrad[:, CUT * g + 128 : CUT * g + 256] = mixed[chip, 64:96, :]
    q = jnp.concatenate([qt[mine, :], qt[other, :]], axis=0)
    hi, mid = split2(q)
    hi, mid = hi.astype(F32), mid.astype(F32)
    ogp = turned(og, t).astype(F32)
    lhs = jnp.concatenate([ogp, -hi, -hi, -mid, -mid], axis=0).T.astype(BF16)
    for c in range(0, WIDE, STEP):
        cols = slice(c, c + STEP)
        chips = range(c // 128, (c + STEP) // 128)
        own = jnp.concatenate([mixed[j, 0:32, :] for j in chips], axis=1)
        oth = jnp.concatenate([roth[j] for j in chips], axis=1)
        fac[mine, cols] = own[0:16]
        fac[other, cols] = oth[0:16]
        high = jnp.concatenate([own[0:16], oth[0:16]], axis=0)
        low = jnp.concatenate([own[16:32], oth[16:32]], axis=0)
        rhs = jnp.concatenate(
            [a[:, cols] for a in (a0, a1, a2, a3)] + [high, low, high, low], axis=0
        )
        total = jnp.dot(lhs, rhs, preferred_element_type=F32) + ef[:, cols].astype(F32)
        err[:, cols] = total.astype(BF16)


def input_kernel(w, feats, r1, r2, r3, out, fv, weights, total, sems):
    cols = pl.ds(pl.multiple_of(plane() * CUT, CUT), CUT)
    pairs = [(w.at[:, cols], weights.at[pl.ds(0, HEAD), :]), (feats, fv)]
    pairs += [
        (r.at[pl.ds(0, HEAD), :], weights.at[pl.ds(HEAD * k, HEAD), :])
        for k, r in enumerate((r1, r2, r3), 1)
    ]
    fetched(pairs, sems)
    for g in range(0, PLANE, 4):
        rows = jnp.concatenate([fv[g + i] for i in range(4)], axis=0)
        part = jnp.dot(rows, weights[...], preferred_element_type=F32).astype(BF16)
        for i in range(4):
            total[g + i] = part[OWN * i : OWN * i + OWN]
    fetched([(total, out)], sems)


def moved(x, k, axis="t"):
    return lax.ppermute(x, axis, [(i, (i + k) % 4) for i in range(4)])


def swapped(x):
    return lax.ppermute(x, "core", [(0, 1), (1, 0)])


def exchanged(x, axes):
    return lax.all_to_all(x, axes, 0, 0, tiled=True)


def local(activations, out_grad, value_weight, error_feedback, warm_right):
    act, og, weight = activations[0], out_grad[0], value_weight[0]
    ef = error_feedback[0, 0]
    warm = warm_right[0, 0].T

    sends = call(
        pack_kernel,
        [((HEAD + 16, CUT), BF16)] * 3,
        [pltpu.VMEM((128, HEAD), BF16), pltpu.SemaphoreType.DMA((4,))],
        space=pltpu.MemorySpace.HBM,
        room=60,
    )(weight, og)
    got = [moved(x, k) for k, x in zip((1, 2, 3), sends)]
    act, got = lax.optimization_barrier((act, got))
    acts = [act] + [moved(act, k) for k in (1, 2, 3)]
    (rows,) = call(rows_kernel, [((PLANE, OWN, 512), BF16)], [pltpu.VMEM((OWN, 512), BF16)])(og, *got)
    feats = exchanged(rows, ("x", "y"))
    inner, fed, lines = call(
        early_kernel,
        [((RANK, OWN), F32), ((RANK, HEAD), F32), ((RANK, WIDE), BF16)],
        flops=10**10,
        moved=10**8,
    )(act, ef, warm)

    half = ((HALF, HEAD), F32)
    left_keep, left_send = call(
        left_kernel, [half, half], [pltpu.VMEM((RANK, HEAD), F32)], flops=5 * 10**7, moved=10**6
    )(*acts[1:], og, lines, inner, fed)
    left_send, feats = lax.optimization_barrier((left_send, feats))

    left_half = left_keep + swapped(left_send)
    pieces = exchanged(jnp.broadcast_to(left_half[None], (N_CHIPS, HALF, HEAD)), CHIPS)
    (inputs,) = call(
        input_kernel,
        [((PLANE, OWN, CUT), BF16)],
        [
            pltpu.VMEM((PLANE, OWN, 512), BF16),
            pltpu.VMEM((512, CUT), BF16),
            pltpu.VMEM((PLANE, OWN, CUT), BF16),
            pltpu.SemaphoreType.DMA((5,)),
        ],
        flops=2 * 10**8,
        moved=2 * 10**6,
        space=pltpu.MemorySpace.HBM,
        dest=pltpu.MemorySpace.HBM,
        room=60,
    )(weight, feats, *got)
    pieces, inputs = lax.optimization_barrier((pieces, inputs))
    left_own = jnp.sum(pieces, axis=0)
    left_other = swapped(left_own)

    block = ((N_CHIPS, HALF, 128), F32)
    basis, right_keep, right_send = call(
        basis_kernel,
        [((RANK, HEAD), F32), block, block],
        [pltpu.VMEM((RANK, HEAD), F32), pltpu.VMEM((RANK, HEAD), F32)],
        flops=10**8,
        moved=3 * 10**6,
    )(left_own, left_other, *acts, og, ef)

    pieces = exchanged(right_keep + swapped(right_send), CHIPS)
    (mixed,) = call(spread_kernel, [((N_CHIPS, 96, 128), BF16)])(pieces, inputs)
    mixed = exchanged(mixed, CHIPS)
    right_other = swapped(mixed[:, 0:32])

    err, fac, igrad = call(
        finish_kernel,
        [((HEAD, WIDE), BF16), ((RANK, WIDE), BF16), ((OWN, WIDE), BF16)],
        flops=3 * 10**8,
        moved=5 * 10**6,
    )(mixed, right_other, basis, og, *acts, ef)

    return (err[None, None], basis.T[None], fac.T[None, None], igrad[None])


def solution(mesh):
    parted = Mesh(
        mesh.devices.reshape(4, 2, 4, 2, 4), EVERY
    )
    return jax.shard_map(
        local,
        mesh=parted,
        in_specs=(
            P(None, EVERY, None),
            P(None, DP, "t"),
            P(None, "t", None),
            P(None, DP, "t", None),
            P(None, "t", None, None),
        ),
        out_specs=(
            P(None, DP, "t", None),
            P(None, "t", None),
            P(None, "t", None, None),
            P(None, EVERY, None),
        ),
        check_vma=False,
    )
```

```python
import jax
import jax.numpy as jnp
from jax import lax
from jax.experimental import pallas as pl
from jax.experimental.pallas import tpu as pltpu
from jax.sharding import Mesh
from jax.sharding import PartitionSpec as P

F32 = jnp.float32
BF16 = jnp.bfloat16
HIGH = lax.Precision.HIGHEST
CHIPS = ("x", "zl", "y")
DP = ("x", "zl", "y", "core")
EVERY = DP + ("t",)

TENSOR = 4
REPLICAS = 64
WIDE = 4096
HEAD = 128
RANK = 32
HALF = RANK // 2
OWN = 32
CUT = 256
PLANE = 16
N_CHIPS = REPLICAS // 2
STEP = 512
NT = (((1,), (1,)), ((), ()))


def split3(x):
    hi = x.astype(BF16)
    rest = x - hi.astype(F32)
    mid = rest.astype(BF16)
    low = (rest - mid.astype(F32)).astype(BF16)
    return (hi, mid, low)


def split2(x):
    hi = x.astype(BF16)
    return (hi, (x - hi.astype(F32)).astype(BF16))


def turned(ref, t):
    blocks = [ref[pl.ds(((t - k + TENSOR) % TENSOR) * OWN, OWN), :] for k in range(TENSOR)]
    return jnp.concatenate(blocks, axis=0)


def call(kernel, outs, scratch=(), flops=10**6, moved=10**6, space=pltpu.VMEM, dest=pltpu.VMEM, room=8):

    def run(*args):
        return pl.pallas_call(
            kernel,
            out_shape=[jax.ShapeDtypeStruct(s, d) for s, d in outs],
            in_specs=[pl.BlockSpec(memory_space=space)] * len(args),
            out_specs=[pl.BlockSpec(memory_space=dest)] * len(outs),
            scratch_shapes=list(scratch),
            compiler_params=pltpu.CompilerParams(vmem_limit_bytes=room * 2**20),
            cost_estimate=pl.CostEstimate(flops=flops, bytes_accessed=moved, transcendentals=0),
        )(*args)

    return run


def fetched(pairs, sems):
    copies = [pltpu.make_async_copy(a, b, sems.at[i]) for i, (a, b) in enumerate(pairs)]
    for copy in copies:
        copy.start()
    for copy in copies:
        copy.wait()


def plane():
    return 4 * lax.axis_index("x") + lax.axis_index("y")


def pack_kernel(w, og, s1, s2, s3, lines, feats, packed, sems):
    t = lax.axis_index("t")
    cols = pl.ds(pl.multiple_of(plane() * CUT, CUT), CUT)
    fetched([(w.at[:, cols], lines), (og, feats)], sems)
    for k in range(1, TENSOR):
        first = OWN * lax.rem(t + k, TENSOR)
        packed[k - 1, 0:HEAD, :] = lines[...]
        for h in range(2):
            rows = pl.ds(pl.multiple_of(first + 16 * h, 16), 16)
            packed[k - 1, HEAD : HEAD + 16, 128 * h : 128 * h + 128] = feats[rows, :]
    fetched([(packed.at[k], send) for k, send in enumerate((s1, s2, s3))], sems)


def rows_kernel(og, r1, r2, r3, out, held):
    t = lax.axis_index("t")
    held[:, 0:128] = og[pl.ds(pl.multiple_of(OWN * t, OWN), OWN), :]
    for k, r in enumerate((r1, r2, r3), 1):
        for h in range(2):
            held[16 * h : 16 * h + 16, 128 * k : 128 * k + 128] = r[
                HEAD : HEAD + 16, 128 * h : 128 * h + 128
            ]
    for g in range(PLANE):
        out[g] = held[...]


def early_kernel(a0, ef, warm, inner, fed, lines):
    lines[...] = warm[...]
    inner[...] = lax.dot_general(warm[...], a0[...], NT, preferred_element_type=F32)
    fed[...] = lax.dot_general(warm[...], ef[...], NT, preferred_element_type=F32)


def left_kernel(a1, a2, a3, og, lines, inner0, fed, keep, send, held):
    t, core = lax.axis_index("t"), lax.axis_index("core")
    ogp = turned(og, t)
    rest = [
        lax.dot_general(lines[...], a[...], NT, preferred_element_type=F32) for a in (a1, a2, a3)
    ]
    inner = jnp.concatenate([inner0[...]] + rest, axis=1)
    prod = jnp.dot(jnp.concatenate(split3(inner), axis=0), ogp, preferred_element_type=F32)
    held[...] = prod[0:RANK] + prod[RANK : 2 * RANK] + prod[2 * RANK :] + fed[...]
    keep[...] = held[pl.ds(pl.multiple_of(core * HALF, HALF), HALF), :]
    send[...] = held[pl.ds(pl.multiple_of((1 - core) * HALF, HALF), HALF), :]


def basis_kernel(lown, loth, a0, a1, a2, a3, og, ef, qt, keep, send, held, heldo):
    t, core = lax.axis_index("t"), lax.axis_index("core")
    mine = pl.ds(pl.multiple_of(core * HALF, HALF), HALF)
    other = pl.ds(pl.multiple_of((1 - core) * HALF, HALF), HALF)
    held[mine, :] = lown[...]
    held[other, :] = loth[...]
    left = held[...]
    gram = lax.dot_general(left, left, NT, precision=HIGH, preferred_element_type=F32)
    row = lax.broadcasted_iota(jnp.int32, (RANK, 1), 0)
    for k in range(RANK - 1):
        scale = 1.0 / gram[k : k + 1, k : k + 1]
        factor = jnp.where(row > k, gram[:, k : k + 1] * scale, 0.0)
        pivot_g, pivot_l = gram[k : k + 1, :], left[k : k + 1, :]
        gram = gram - factor * pivot_g
        left = left - factor * pivot_l
    eye = row == lax.broadcasted_iota(jnp.int32, (RANK, RANK), 1)
    diagonal = jnp.sum(jnp.where(eye, gram, 0.0), axis=1, keepdims=True)
    basis = left * (1.0 / jnp.sqrt(diagonal))
    qt[...] = basis
    ogp = turned(og, t)
    prod = lax.dot_general(
        jnp.concatenate(split3(basis), axis=0), ogp, NT, preferred_element_type=F32
    )
    held[...] = basis
    heldo[...] = prod[0:RANK] + prod[RANK : 2 * RANK] + prod[2 * RANK :]
    q = jnp.concatenate([held[mine, :], held[other, :]], axis=0)
    qo = jnp.concatenate([heldo[mine, :], heldo[other, :]], axis=0)
    lhs = jnp.concatenate(
        [jnp.concatenate(split3(qo), axis=0), jnp.concatenate(split3(q), axis=0)], axis=1
    )
    for c in range(0, WIDE, STEP):
        cols = slice(c, c + STEP)
        rhs = jnp.concatenate([a[:, cols] for a in (a0, a1, a2, a3, ef)], axis=0)
        p = jnp.dot(lhs, rhs, preferred_element_type=F32)
        r = p[0:RANK] + p[RANK : 2 * RANK] + p[2 * RANK :]
        for j in range(STEP // 128):
            chip = c // 128 + j
            keep[chip] = r[0:HALF, 128 * j : 128 * j + 128]
            send[chip] = r[HALF:, 128 * j : 128 * j + 128]


def spread_kernel(pieces, inputs, out):
    hi, mid = split2(jnp.sum(pieces[...], axis=0) * (1.0 / REPLICAS))
    for chip in range(N_CHIPS):
        g = chip // 8 * 4 + chip % 4
        out[chip, 0:16, :] = hi
        out[chip, 16:32, :] = mid
        out[chip, 32:64, :] = inputs[g, :, 0:128]
        out[chip, 64:96, :] = inputs[g, :, 128:256]


def finish_kernel(mixed, roth, qt, og, a0, a1, a2, a3, ef, err, fac, igrad):
    t, core = lax.axis_index("t"), lax.axis_index("core")
    zl = lax.axis_index("zl")
    mine = pl.ds(pl.multiple_of(core * HALF, HALF), HALF)
    other = pl.ds(pl.multiple_of((1 - core) * HALF, HALF), HALF)
    for g in range(PLANE):
        chip = g // 4 * 8 + 4 * zl + g % 4
        igrad[:, CUT * g : CUT * g + 128] = mixed[chip, 32:64, :]
        igrad[:, CUT * g + 128 : CUT * g + 256] = mixed[chip, 64:96, :]
    q = jnp.concatenate([qt[mine, :], qt[other, :]], axis=0)
    hi, mid = split2(q)
    hi, mid = hi.astype(F32), mid.astype(F32)
    ogp = turned(og, t).astype(F32)
    lhs = jnp.concatenate([ogp, -hi, -hi, -mid, -mid], axis=0).T.astype(BF16)
    for c in range(0, WIDE, STEP):
        cols = slice(c, c + STEP)
        chips = range(c // 128, (c + STEP) // 128)
        own = jnp.concatenate([mixed[j, 0:32, :] for j in chips], axis=1)
        oth = jnp.concatenate([roth[j] for j in chips], axis=1)
        fac[mine, cols] = own[0:16]
        fac[other, cols] = oth[0:16]
        high = jnp.concatenate([own[0:16], oth[0:16]], axis=0)
        low = jnp.concatenate([own[16:32], oth[16:32]], axis=0)
        rhs = jnp.concatenate(
            [a[:, cols] for a in (a0, a1, a2, a3)] + [high, low, high, low], axis=0
        )
        total = jnp.dot(lhs, rhs, preferred_element_type=F32) + ef[:, cols].astype(F32)
        err[:, cols] = total.astype(BF16)


def input_kernel(w, feats, r1, r2, r3, out, fv, weights, total, sems):
    cols = pl.ds(pl.multiple_of(plane() * CUT, CUT), CUT)
    pairs = [(w.at[:, cols], weights.at[pl.ds(0, HEAD), :]), (feats, fv)]
    pairs += [
        (r.at[pl.ds(0, HEAD), :], weights.at[pl.ds(HEAD * k, HEAD), :])
        for k, r in enumerate((r1, r2, r3), 1)
    ]
    fetched(pairs, sems)
    for g in range(0, PLANE, 4):
        rows = jnp.concatenate([fv[g + i] for i in range(4)], axis=0)
        part = jnp.dot(rows, weights[...], preferred_element_type=F32).astype(BF16)
        for i in range(4):
            total[g + i] = part[OWN * i : OWN * i + OWN]
    fetched([(total, out)], sems)


def moved(x, k, axis="t"):
    return lax.ppermute(x, axis, [(i, (i + k) % 4) for i in range(4)])


def swapped(x):
    return lax.ppermute(x, "core", [(0, 1), (1, 0)])


def exchanged(x, axes):
    return lax.all_to_all(x, axes, 0, 0, tiled=True)


def local(activations, out_grad, value_weight, error_feedback, warm_right):
    act, og, weight = activations[0], out_grad[0], value_weight[0]
    ef = error_feedback[0, 0]
    warm = warm_right[0, 0].T

    sends = call(
        pack_kernel,
        [((HEAD + 16, CUT), BF16)] * 3,
        [
            pltpu.VMEM((HEAD, CUT), BF16),
            pltpu.VMEM((128, HEAD), BF16),
            pltpu.VMEM((3, HEAD + 16, CUT), BF16),
            pltpu.SemaphoreType.DMA((3,)),
        ],
        space=pltpu.MemorySpace.HBM,
        dest=pltpu.MemorySpace.HBM,
        room=60,
    )(weight, og)
    got = [moved(x, k) for k, x in zip((1, 2, 3), sends)]
    acts = [act] + [moved(act, k) for k in (1, 2, 3)]
    (rows,) = call(rows_kernel, [((PLANE, OWN, 512), BF16)], [pltpu.VMEM((OWN, 512), BF16)])(og, *got)
    feats = exchanged(rows, ("x", "y"))
    inner, fed, lines = call(
        early_kernel,
        [((RANK, OWN), F32), ((RANK, HEAD), F32), ((RANK, WIDE), BF16)],
        flops=10**10,
        moved=10**8,
    )(act, ef, warm)

    (inputs,) = call(
        input_kernel,
        [((PLANE, OWN, CUT), BF16)],
        [
            pltpu.VMEM((PLANE, OWN, 512), BF16),
            pltpu.VMEM((512, CUT), BF16),
            pltpu.VMEM((PLANE, OWN, CUT), BF16),
            pltpu.SemaphoreType.DMA((5,)),
        ],
        flops=2 * 10**8,
        moved=2 * 10**6,
        space=pltpu.MemorySpace.HBM,
        dest=pltpu.MemorySpace.HBM,
        room=60,
    )(weight, feats, *got)
    lines, inputs = lax.optimization_barrier((lines, inputs))
    half = ((HALF, HEAD), F32)
    left_keep, left_send = call(
        left_kernel, [half, half], [pltpu.VMEM((RANK, HEAD), F32)], flops=5 * 10**7, moved=10**6
    )(*acts[1:], og, lines, inner, fed)

    left_half = left_keep + swapped(left_send)
    pieces = exchanged(jnp.broadcast_to(left_half[None], (N_CHIPS, HALF, HEAD)), CHIPS)
    left_own = jnp.sum(pieces, axis=0)
    left_other = swapped(left_own)

    block = ((N_CHIPS, HALF, 128), F32)
    basis, right_keep, right_send = call(
        basis_kernel,
        [((RANK, HEAD), F32), block, block],
        [pltpu.VMEM((RANK, HEAD), F32), pltpu.VMEM((RANK, HEAD), F32)],
        flops=10**8,
        moved=3 * 10**6,
    )(left_own, left_other, *acts, og, ef)

    pieces = exchanged(right_keep + swapped(right_send), CHIPS)
    (mixed,) = call(spread_kernel, [((N_CHIPS, 96, 128), BF16)])(pieces, inputs)
    mixed = exchanged(mixed, CHIPS)
    right_other = swapped(mixed[:, 0:32])

    err, fac, igrad = call(
        finish_kernel,
        [((HEAD, WIDE), BF16), ((RANK, WIDE), BF16), ((OWN, WIDE), BF16)],
        flops=3 * 10**8,
        moved=5 * 10**6,
    )(mixed, right_other, basis, og, *acts, ef)

    return (err[None, None], basis.T[None], fac.T[None, None], igrad[None])


def solution(mesh):
    parted = Mesh(
        mesh.devices.reshape(4, 2, 4, 2, 4), EVERY
    )
    return jax.shard_map(
        local,
        mesh=parted,
        in_specs=(
            P(None, EVERY, None),
            P(None, DP, "t"),
            P(None, "t", None),
            P(None, DP, "t", None),
            P(None, "t", None, None),
        ),
        out_specs=(
            P(None, DP, "t", None),
            P(None, "t", None),
            P(None, "t", None, None),
            P(None, EVERY, None),
        ),
        check_vma=False,
    )
```

```python
import jax
import jax.numpy as jnp
from jax import lax
from jax.experimental import pallas as pl
from jax.experimental.pallas import tpu as pltpu
from jax.sharding import Mesh
from jax.sharding import PartitionSpec as P

F32 = jnp.float32
BF16 = jnp.bfloat16
HIGH = lax.Precision.HIGHEST
CHIPS = ("x", "zl", "y")
DP = ("x", "zl", "y", "core")
EVERY = DP + ("t",)

TENSOR = 4
REPLICAS = 64
WIDE = 4096
HEAD = 128
RANK = 32
HALF = RANK // 2
OWN = 32
CUT = 256
PLANE = 16
N_CHIPS = REPLICAS // 2
STEP = 512
NT = (((1,), (1,)), ((), ()))


def split3(x):
    hi = x.astype(BF16)
    rest = x - hi.astype(F32)
    mid = rest.astype(BF16)
    low = (rest - mid.astype(F32)).astype(BF16)
    return (hi, mid, low)


def split2(x):
    hi = x.astype(BF16)
    return (hi, (x - hi.astype(F32)).astype(BF16))


def turned(ref, t):
    blocks = [ref[pl.ds(((t - k + TENSOR) % TENSOR) * OWN, OWN), :] for k in range(TENSOR)]
    return jnp.concatenate(blocks, axis=0)


def call(kernel, outs, scratch=(), flops=10**6, moved=10**6, space=pltpu.VMEM, dest=pltpu.VMEM, room=8):

    def run(*args):
        return pl.pallas_call(
            kernel,
            out_shape=[jax.ShapeDtypeStruct(s, d) for s, d in outs],
            in_specs=[pl.BlockSpec(memory_space=space)] * len(args),
            out_specs=[pl.BlockSpec(memory_space=dest)] * len(outs),
            scratch_shapes=list(scratch),
            compiler_params=pltpu.CompilerParams(vmem_limit_bytes=room * 2**20),
            cost_estimate=pl.CostEstimate(flops=flops, bytes_accessed=moved, transcendentals=0),
        )(*args)

    return run


def fetched(pairs, sems):
    copies = [pltpu.make_async_copy(a, b, sems.at[i]) for i, (a, b) in enumerate(pairs)]
    for copy in copies:
        copy.start()
    for copy in copies:
        copy.wait()


def plane():
    return 4 * lax.axis_index("x") + lax.axis_index("y")


def pack_kernel(w, og, s1, s2, s3, feats, sems):
    t, core = lax.axis_index("t"), lax.axis_index("core")
    cols = pl.ds(pl.multiple_of(plane() * CUT, CUT), CUT)
    part = w.at[pl.ds(pl.multiple_of(core * 64, 64), 64), cols]
    sends = (s1, s2, s3)
    fetched([(part, s.at[pl.ds(0, 64), :]) for s in sends] + [(og, feats)], sems)
    for k, send in enumerate(sends, 1):
        first = OWN * lax.rem(t + k, TENSOR)
        for h in range(2):
            rows = pl.ds(pl.multiple_of(first + 16 * h, 16), 16)
            send[64:80, 128 * h : 128 * h + 128] = feats[rows, :]


def rows_kernel(og, r1, r2, r3, out, held):
    t = lax.axis_index("t")
    held[:, 0:128] = og[pl.ds(pl.multiple_of(OWN * t, OWN), OWN), :]
    for k, r in enumerate((r1, r2, r3), 1):
        for h in range(2):
            held[16 * h : 16 * h + 16, 128 * k : 128 * k + 128] = r[
                64:80, 128 * h : 128 * h + 128
            ]
    for g in range(PLANE):
        out[g] = held[...]


def early_kernel(a0, ef, warm, inner, fed, lines):
    lines[...] = warm[...]
    inner[...] = lax.dot_general(warm[...], a0[...], NT, preferred_element_type=F32)
    fed[...] = lax.dot_general(warm[...], ef[...], NT, preferred_element_type=F32)


def left_kernel(a1, a2, a3, og, lines, inner0, fed, keep, send, held):
    t, core = lax.axis_index("t"), lax.axis_index("core")
    ogp = turned(og, t)
    rest = [
        lax.dot_general(lines[...], a[...], NT, preferred_element_type=F32) for a in (a1, a2, a3)
    ]
    inner = jnp.concatenate([inner0[...]] + rest, axis=1)
    prod = jnp.dot(jnp.concatenate(split3(inner), axis=0), ogp, preferred_element_type=F32)
    held[...] = prod[0:RANK] + prod[RANK : 2 * RANK] + prod[2 * RANK :] + fed[...]
    keep[...] = held[pl.ds(pl.multiple_of(core * HALF, HALF), HALF), :]
    send[...] = held[pl.ds(pl.multiple_of((1 - core) * HALF, HALF), HALF), :]


def basis_kernel(lown, loth, a0, a1, a2, a3, og, ef, qt, keep, send, held, heldo):
    t, core = lax.axis_index("t"), lax.axis_index("core")
    mine = pl.ds(pl.multiple_of(core * HALF, HALF), HALF)
    other = pl.ds(pl.multiple_of((1 - core) * HALF, HALF), HALF)
    held[mine, :] = lown[...]
    held[other, :] = loth[...]
    left = held[...]
    gram = lax.dot_general(left, left, NT, precision=HIGH, preferred_element_type=F32)
    row = lax.broadcasted_iota(jnp.int32, (RANK, 1), 0)
    for k in range(RANK - 1):
        scale = 1.0 / gram[k : k + 1, k : k + 1]
        factor = jnp.where(row > k, gram[:, k : k + 1] * scale, 0.0)
        pivot_g, pivot_l = gram[k : k + 1, :], left[k : k + 1, :]
        gram = gram - factor * pivot_g
        left = left - factor * pivot_l
    eye = row == lax.broadcasted_iota(jnp.int32, (RANK, RANK), 1)
    diagonal = jnp.sum(jnp.where(eye, gram, 0.0), axis=1, keepdims=True)
    basis = left * (1.0 / jnp.sqrt(diagonal))
    qt[...] = basis
    ogp = turned(og, t)
    prod = lax.dot_general(
        jnp.concatenate(split3(basis), axis=0), ogp, NT, preferred_element_type=F32
    )
    held[...] = basis
    heldo[...] = prod[0:RANK] + prod[RANK : 2 * RANK] + prod[2 * RANK :]
    q = jnp.concatenate([held[mine, :], held[other, :]], axis=0)
    qo = jnp.concatenate([heldo[mine, :], heldo[other, :]], axis=0)
    lhs = jnp.concatenate(
        [jnp.concatenate(split3(qo), axis=0), jnp.concatenate(split3(q), axis=0)], axis=1
    )
    for c in range(0, WIDE, STEP):
        cols = slice(c, c + STEP)
        rhs = jnp.concatenate([a[:, cols] for a in (a0, a1, a2, a3, ef)], axis=0)
        p = jnp.dot(lhs, rhs, preferred_element_type=F32)
        r = p[0:RANK] + p[RANK : 2 * RANK] + p[2 * RANK :]
        for j in range(STEP // 128):
            chip = c // 128 + j
            keep[chip] = r[0:HALF, 128 * j : 128 * j + 128]
            send[chip] = r[HALF:, 128 * j : 128 * j + 128]


def spread_kernel(pieces, inputs, out):
    hi, mid = split2(jnp.sum(pieces[...], axis=0) * (1.0 / REPLICAS))
    for chip in range(N_CHIPS):
        g = chip // 8 * 4 + chip % 4
        out[chip, 0:16, :] = hi
        out[chip, 16:32, :] = mid
        out[chip, 32:64, :] = inputs[g, :, 0:128]
        out[chip, 64:96, :] = inputs[g, :, 128:256]


def finish_kernel(mixed, roth, qt, og, a0, a1, a2, a3, ef, err, fac, igrad):
    t, core = lax.axis_index("t"), lax.axis_index("core")
    zl = lax.axis_index("zl")
    mine = pl.ds(pl.multiple_of(core * HALF, HALF), HALF)
    other = pl.ds(pl.multiple_of((1 - core) * HALF, HALF), HALF)
    for g in range(PLANE):
        chip = g // 4 * 8 + 4 * zl + g % 4
        igrad[:, CUT * g : CUT * g + 128] = mixed[chip, 32:64, :]
        igrad[:, CUT * g + 128 : CUT * g + 256] = mixed[chip, 64:96, :]
    q = jnp.concatenate([qt[mine, :], qt[other, :]], axis=0)
    hi, mid = split2(q)
    hi, mid = hi.astype(F32), mid.astype(F32)
    ogp = turned(og, t).astype(F32)
    lhs = jnp.concatenate([ogp, -hi, -hi, -mid, -mid], axis=0).T.astype(BF16)
    for c in range(0, WIDE, STEP):
        cols = slice(c, c + STEP)
        chips = range(c // 128, (c + STEP) // 128)
        own = jnp.concatenate([mixed[j, 0:32, :] for j in chips], axis=1)
        oth = jnp.concatenate([roth[j] for j in chips], axis=1)
        fac[mine, cols] = own[0:16]
        fac[other, cols] = oth[0:16]
        high = jnp.concatenate([own[0:16], oth[0:16]], axis=0)
        low = jnp.concatenate([own[16:32], oth[16:32]], axis=0)
        rhs = jnp.concatenate(
            [a[:, cols] for a in (a0, a1, a2, a3)] + [high, low, high, low], axis=0
        )
        total = jnp.dot(lhs, rhs, preferred_element_type=F32) + ef[:, cols].astype(F32)
        err[:, cols] = total.astype(BF16)


def input_kernel(w, feats, r1, r2, r3, c1, c2, c3, out, fv, weights, total, sems):
    core = lax.axis_index("core")
    cols = pl.ds(pl.multiple_of(plane() * CUT, CUT), CUT)
    pairs = [(w.at[:, cols], weights.at[pl.ds(0, HEAD), :]), (feats, fv)]
    for k, (r, c) in enumerate(((r1, c1), (r2, c2), (r3, c3)), 1):
        for source, side in ((r, core), (c, 1 - core)):
            rows = pl.ds(pl.multiple_of(HEAD * k + 64 * side, 64), 64)
            pairs.append((source.at[pl.ds(0, 64), :], weights.at[rows, :]))
    fetched(pairs, sems)
    for g in range(0, PLANE, 4):
        rows = jnp.concatenate([fv[g + i] for i in range(4)], axis=0)
        part = jnp.dot(rows, weights[...], preferred_element_type=F32).astype(BF16)
        for i in range(4):
            total[g + i] = part[OWN * i : OWN * i + OWN]
    fetched([(total, out)], sems)


def moved(x, k, axis="t"):
    return lax.ppermute(x, axis, [(i, (i + k) % 4) for i in range(4)])


def swapped(x):
    return lax.ppermute(x, "core", [(0, 1), (1, 0)])


def exchanged(x, axes):
    return lax.all_to_all(x, axes, 0, 0, tiled=True)


def local(activations, out_grad, value_weight, error_feedback, warm_right):
    act, og, weight = activations[0], out_grad[0], value_weight[0]
    ef = error_feedback[0, 0]
    warm = warm_right[0, 0].T

    sends = call(
        pack_kernel,
        [((80, CUT), BF16)] * 3,
        [pltpu.VMEM((128, HEAD), BF16), pltpu.SemaphoreType.DMA((4,))],
        space=pltpu.MemorySpace.HBM,
        room=60,
    )(weight, og)
    got = [moved(x, k) for k, x in zip((1, 2, 3), sends)]
    acts = [act] + [moved(act, k) for k in (1, 2, 3)]
    (rows,) = call(rows_kernel, [((PLANE, OWN, 512), BF16)], [pltpu.VMEM((OWN, 512), BF16)])(og, *got)
    feats = exchanged(rows, ("x", "y"))
    inner, fed, lines = call(
        early_kernel,
        [((RANK, OWN), F32), ((RANK, HEAD), F32), ((RANK, WIDE), BF16)],
        flops=10**10,
        moved=10**8,
    )(act, ef, warm)

    half = ((HALF, HEAD), F32)
    left_keep, left_send = call(
        left_kernel, [half, half], [pltpu.VMEM((RANK, HEAD), F32)], flops=5 * 10**7, moved=10**6
    )(*acts[1:], og, lines, inner, fed)
    left_send, feats = lax.optimization_barrier((left_send, feats))

    left_half = left_keep + swapped(left_send)
    left_half, got = lax.optimization_barrier((left_half, got))
    traded = [swapped(g) for g in got]
    pieces = exchanged(jnp.broadcast_to(left_half[None], (N_CHIPS, HALF, HEAD)), CHIPS)
    (inputs,) = call(
        input_kernel,
        [((PLANE, OWN, CUT), BF16)],
        [
            pltpu.VMEM((PLANE, OWN, 512), BF16),
            pltpu.VMEM((512, CUT), BF16),
            pltpu.VMEM((PLANE, OWN, CUT), BF16),
            pltpu.SemaphoreType.DMA((8,)),
        ],
        flops=2 * 10**8,
        moved=2 * 10**6,
        space=pltpu.MemorySpace.HBM,
        dest=pltpu.MemorySpace.HBM,
        room=60,
    )(weight, feats, *got, *traded)
    pieces, inputs = lax.optimization_barrier((pieces, inputs))
    left_own = jnp.sum(pieces, axis=0)
    left_other = swapped(left_own)

    block = ((N_CHIPS, HALF, 128), F32)
    basis, right_keep, right_send = call(
        basis_kernel,
        [((RANK, HEAD), F32), block, block],
        [pltpu.VMEM((RANK, HEAD), F32), pltpu.VMEM((RANK, HEAD), F32)],
        flops=10**8,
        moved=3 * 10**6,
    )(left_own, left_other, *acts, og, ef)

    pieces = exchanged(right_keep + swapped(right_send), CHIPS)
    (mixed,) = call(spread_kernel, [((N_CHIPS, 96, 128), BF16)])(pieces, inputs)
    mixed = exchanged(mixed, CHIPS)
    right_other = swapped(mixed[:, 0:32])

    err, fac, igrad = call(
        finish_kernel,
        [((HEAD, WIDE), BF16), ((RANK, WIDE), BF16), ((OWN, WIDE), BF16)],
        flops=3 * 10**8,
        moved=5 * 10**6,
    )(mixed, right_other, basis, og, *acts, ef)

    return (err[None, None], basis.T[None], fac.T[None, None], igrad[None])


def solution(mesh):
    parted = Mesh(
        mesh.devices.reshape(4, 2, 4, 2, 4), EVERY
    )
    return jax.shard_map(
        local,
        mesh=parted,
        in_specs=(
            P(None, EVERY, None),
            P(None, DP, "t"),
            P(None, "t", None),
            P(None, DP, "t", None),
            P(None, "t", None, None),
        ),
        out_specs=(
            P(None, DP, "t", None),
            P(None, "t", None),
            P(None, "t", None, None),
            P(None, EVERY, None),
        ),
        check_vma=False,
    )
```

```python
import jax
import jax.numpy as jnp
from jax import lax
from jax.experimental import pallas as pl
from jax.experimental.pallas import tpu as pltpu
from jax.sharding import Mesh
from jax.sharding import PartitionSpec as P

F32 = jnp.float32
BF16 = jnp.bfloat16
HIGH = lax.Precision.HIGHEST
CHIPS = ("x", "zl", "y")
DP = ("x", "zl", "y", "core")
EVERY = DP + ("t",)

TENSOR = 4
REPLICAS = 64
WIDE = 4096
HEAD = 128
RANK = 32
HALF = RANK // 2
OWN = 32
CUT = 256
PLANE = 16
N_CHIPS = REPLICAS // 2
STEP = 512
NT = (((1,), (1,)), ((), ()))


def split3(x):
    hi = x.astype(BF16)
    rest = x - hi.astype(F32)
    mid = rest.astype(BF16)
    low = (rest - mid.astype(F32)).astype(BF16)
    return (hi, mid, low)


def split2(x):
    hi = x.astype(BF16)
    return (hi, (x - hi.astype(F32)).astype(BF16))


def turned(ref, t):
    blocks = [ref[pl.ds(((t - k + TENSOR) % TENSOR) * OWN, OWN), :] for k in range(TENSOR)]
    return jnp.concatenate(blocks, axis=0)


def call(kernel, outs, scratch=(), flops=10**6, moved=10**6, space=pltpu.VMEM, dest=pltpu.VMEM, room=8):

    def run(*args):
        return pl.pallas_call(
            kernel,
            out_shape=[jax.ShapeDtypeStruct(s, d) for s, d in outs],
            in_specs=[pl.BlockSpec(memory_space=space)] * len(args),
            out_specs=[pl.BlockSpec(memory_space=dest)] * len(outs),
            scratch_shapes=list(scratch),
            compiler_params=pltpu.CompilerParams(vmem_limit_bytes=room * 2**20),
            cost_estimate=pl.CostEstimate(flops=flops, bytes_accessed=moved, transcendentals=0),
        )(*args)

    return run


def fetched(pairs, sems):
    copies = [pltpu.make_async_copy(a, b, sems.at[i]) for i, (a, b) in enumerate(pairs)]
    for copy in copies:
        copy.start()
    for copy in copies:
        copy.wait()


def plane():
    return 4 * lax.axis_index("x") + lax.axis_index("y")


def pack_kernel(w, og, s1, s2, s3, feats, sems):
    t, core = lax.axis_index("t"), lax.axis_index("core")
    cols = pl.ds(pl.multiple_of(plane() * CUT, CUT), CUT)
    part = w.at[pl.ds(pl.multiple_of(core * 64, 64), 64), cols]
    sends = (s1, s2, s3)
    fetched([(part, s.at[pl.ds(0, 64), :]) for s in sends] + [(og, feats)], sems)
    for k, send in enumerate(sends, 1):
        first = OWN * lax.rem(t + k, TENSOR)
        for h in range(2):
            rows = pl.ds(pl.multiple_of(first + 16 * h, 16), 16)
            send[64:80, 128 * h : 128 * h + 128] = feats[rows, :]


def rows_kernel(og, r1, r2, r3, out, held):
    t = lax.axis_index("t")
    held[:, 0:128] = og[pl.ds(pl.multiple_of(OWN * t, OWN), OWN), :]
    for k, r in enumerate((r1, r2, r3), 1):
        for h in range(2):
            held[16 * h : 16 * h + 16, 128 * k : 128 * k + 128] = r[
                64:80, 128 * h : 128 * h + 128
            ]
    for g in range(PLANE):
        out[g] = held[...]


def early_kernel(a0, ef, warm, inner, fed, lines):
    lines[...] = warm[...]
    inner[...] = lax.dot_general(warm[...], a0[...], NT, preferred_element_type=F32)
    fed[...] = lax.dot_general(warm[...], ef[...], NT, preferred_element_type=F32)


def left_kernel(a1, a2, a3, og, lines, inner0, fed, keep, send, held):
    t, core = lax.axis_index("t"), lax.axis_index("core")
    ogp = turned(og, t)
    rest = [
        lax.dot_general(lines[...], a[...], NT, preferred_element_type=F32) for a in (a1, a2, a3)
    ]
    inner = jnp.concatenate([inner0[...]] + rest, axis=1)
    prod = jnp.dot(jnp.concatenate(split3(inner), axis=0), ogp, preferred_element_type=F32)
    held[...] = prod[0:RANK] + prod[RANK : 2 * RANK] + prod[2 * RANK :] + fed[...]
    keep[...] = held[pl.ds(pl.multiple_of(core * HALF, HALF), HALF), :]
    send[...] = held[pl.ds(pl.multiple_of((1 - core) * HALF, HALF), HALF), :]


def basis_kernel(lown, loth, a0, a1, a2, a3, og, ef, qt, keep, send, held, heldo):
    t, core = lax.axis_index("t"), lax.axis_index("core")
    mine = pl.ds(pl.multiple_of(core * HALF, HALF), HALF)
    other = pl.ds(pl.multiple_of((1 - core) * HALF, HALF), HALF)
    held[mine, :] = lown[...]
    held[other, :] = loth[...]
    left = held[...]
    gram = lax.dot_general(left, left, NT, precision=HIGH, preferred_element_type=F32)
    row = lax.broadcasted_iota(jnp.int32, (RANK, 1), 0)
    for k in range(RANK - 1):
        scale = 1.0 / gram[k : k + 1, k : k + 1]
        factor = jnp.where(row > k, gram[:, k : k + 1] * scale, 0.0)
        pivot_g, pivot_l = gram[k : k + 1, :], left[k : k + 1, :]
        gram = gram - factor * pivot_g
        left = left - factor * pivot_l
    eye = row == lax.broadcasted_iota(jnp.int32, (RANK, RANK), 1)
    diagonal = jnp.sum(jnp.where(eye, gram, 0.0), axis=1, keepdims=True)
    basis = left * (1.0 / jnp.sqrt(diagonal))
    qt[...] = basis
    ogp = turned(og, t)
    prod = lax.dot_general(
        jnp.concatenate(split3(basis), axis=0), ogp, NT, preferred_element_type=F32
    )
    held[...] = basis
    heldo[...] = prod[0:RANK] + prod[RANK : 2 * RANK] + prod[2 * RANK :]
    q = jnp.concatenate([held[mine, :], held[other, :]], axis=0)
    qo = jnp.concatenate([heldo[mine, :], heldo[other, :]], axis=0)
    lhs = jnp.concatenate(
        [jnp.concatenate(split3(qo), axis=0), jnp.concatenate(split3(q), axis=0)], axis=1
    )
    for c in range(0, WIDE, STEP):
        cols = slice(c, c + STEP)
        rhs = jnp.concatenate([a[:, cols] for a in (a0, a1, a2, a3, ef)], axis=0)
        p = jnp.dot(lhs, rhs, preferred_element_type=F32)
        r = p[0:RANK] + p[RANK : 2 * RANK] + p[2 * RANK :]
        for j in range(STEP // 128):
            chip = c // 128 + j
            keep[chip] = r[0:HALF, 128 * j : 128 * j + 128]
            send[chip] = r[HALF:, 128 * j : 128 * j + 128]


def spread_kernel(pieces, inputs, out):
    hi, mid = split2(jnp.sum(pieces[...], axis=0) * (1.0 / REPLICAS))
    for chip in range(N_CHIPS):
        g = chip // 8 * 4 + chip % 4
        out[chip, 0:16, :] = hi
        out[chip, 16:32, :] = mid
        out[chip, 32:64, :] = inputs[g, :, 0:128]
        out[chip, 64:96, :] = inputs[g, :, 128:256]


def finish_kernel(mixed, roth, qt, og, a0, a1, a2, a3, ef, err, fac, igrad):
    t, core = lax.axis_index("t"), lax.axis_index("core")
    zl = lax.axis_index("zl")
    mine = pl.ds(pl.multiple_of(core * HALF, HALF), HALF)
    other = pl.ds(pl.multiple_of((1 - core) * HALF, HALF), HALF)
    for g in range(PLANE):
        chip = g // 4 * 8 + 4 * zl + g % 4
        igrad[:, CUT * g : CUT * g + 128] = mixed[chip, 32:64, :]
        igrad[:, CUT * g + 128 : CUT * g + 256] = mixed[chip, 64:96, :]
    q = jnp.concatenate([qt[mine, :], qt[other, :]], axis=0)
    hi, mid = split2(q)
    hi, mid = hi.astype(F32), mid.astype(F32)
    ogp = turned(og, t).astype(F32)
    lhs = jnp.concatenate([ogp, -hi, -hi, -mid, -mid], axis=0).T.astype(BF16)
    for c in range(0, WIDE, STEP):
        cols = slice(c, c + STEP)
        chips = range(c // 128, (c + STEP) // 128)
        own = jnp.concatenate([mixed[j, 0:32, :] for j in chips], axis=1)
        oth = jnp.concatenate([roth[j] for j in chips], axis=1)
        fac[mine, cols] = own[0:16]
        fac[other, cols] = oth[0:16]
        high = jnp.concatenate([own[0:16], oth[0:16]], axis=0)
        low = jnp.concatenate([own[16:32], oth[16:32]], axis=0)
        rhs = jnp.concatenate(
            [a[:, cols] for a in (a0, a1, a2, a3)] + [high, low, high, low], axis=0
        )
        total = jnp.dot(lhs, rhs, preferred_element_type=F32) + ef[:, cols].astype(F32)
        err[:, cols] = total.astype(BF16)


def input_kernel(w, feats, r1, r2, r3, c1, c2, c3, out, fv, weights, total, sems):
    core = lax.axis_index("core")
    cols = pl.ds(pl.multiple_of(plane() * CUT, CUT), CUT)
    pairs = [(w.at[:, cols], weights.at[pl.ds(0, HEAD), :]), (feats, fv)]
    for k, (r, c) in enumerate(((r1, c1), (r2, c2), (r3, c3)), 1):
        for source, side in ((r, core), (c, 1 - core)):
            rows = pl.ds(pl.multiple_of(HEAD * k + 64 * side, 64), 64)
            pairs.append((source.at[pl.ds(0, 64), :], weights.at[rows, :]))
    fetched(pairs, sems)
    for g in range(0, PLANE, 4):
        rows = jnp.concatenate([fv[g + i] for i in range(4)], axis=0)
        part = jnp.dot(rows, weights[...], preferred_element_type=F32).astype(BF16)
        for i in range(4):
            total[g + i] = part[OWN * i : OWN * i + OWN]
    fetched([(total, out)], sems)


def moved(x, k, axis="t"):
    return lax.ppermute(x, axis, [(i, (i + k) % 4) for i in range(4)])


def swapped(x):
    return lax.ppermute(x, "core", [(0, 1), (1, 0)])


def exchanged(x, axes):
    return lax.all_to_all(x, axes, 0, 0, tiled=True)


def local(activations, out_grad, value_weight, error_feedback, warm_right):
    act, og, weight = activations[0], out_grad[0], value_weight[0]
    ef = error_feedback[0, 0]
    warm = warm_right[0, 0].T

    sends = call(
        pack_kernel,
        [((80, CUT), BF16)] * 3,
        [pltpu.VMEM((128, HEAD), BF16), pltpu.SemaphoreType.DMA((4,))],
        space=pltpu.MemorySpace.HBM,
        room=60,
    )(weight, og)
    got = [moved(x, k) for k, x in zip((1, 2, 3), sends)]
    acts = [act] + [moved(act, k) for k in (1, 2, 3)]
    (rows,) = call(rows_kernel, [((PLANE, OWN, 512), BF16)], [pltpu.VMEM((OWN, 512), BF16)])(og, *got)
    feats = exchanged(rows, ("x", "y"))
    inner, fed, lines = call(
        early_kernel,
        [((RANK, OWN), F32), ((RANK, HEAD), F32), ((RANK, WIDE), BF16)],
        flops=10**10,
        moved=10**8,
    )(act, ef, warm)

    got, inner = lax.optimization_barrier((got, inner))
    traded = [swapped(g) for g in got]
    (inputs,) = call(
        input_kernel,
        [((PLANE, OWN, CUT), BF16)],
        [
            pltpu.VMEM((PLANE, OWN, 512), BF16),
            pltpu.VMEM((512, CUT), BF16),
            pltpu.VMEM((PLANE, OWN, CUT), BF16),
            pltpu.SemaphoreType.DMA((8,)),
        ],
        flops=2 * 10**8,
        moved=2 * 10**6,
        space=pltpu.MemorySpace.HBM,
        dest=pltpu.MemorySpace.HBM,
        room=60,
    )(weight, feats, *got, *traded)
    lines, inputs = lax.optimization_barrier((lines, inputs))
    half = ((HALF, HEAD), F32)
    left_keep, left_send = call(
        left_kernel, [half, half], [pltpu.VMEM((RANK, HEAD), F32)], flops=5 * 10**7, moved=10**6
    )(*acts[1:], og, lines, inner, fed)

    left_half = left_keep + swapped(left_send)
    pieces = exchanged(jnp.broadcast_to(left_half[None], (N_CHIPS, HALF, HEAD)), CHIPS)
    left_own = jnp.sum(pieces, axis=0)
    left_other = swapped(left_own)

    block = ((N_CHIPS, HALF, 128), F32)
    basis, right_keep, right_send = call(
        basis_kernel,
        [((RANK, HEAD), F32), block, block],
        [pltpu.VMEM((RANK, HEAD), F32), pltpu.VMEM((RANK, HEAD), F32)],
        flops=10**8,
        moved=3 * 10**6,
    )(left_own, left_other, *acts, og, ef)

    pieces = exchanged(right_keep + swapped(right_send), CHIPS)
    (mixed,) = call(spread_kernel, [((N_CHIPS, 96, 128), BF16)])(pieces, inputs)
    mixed = exchanged(mixed, CHIPS)
    right_other = swapped(mixed[:, 0:32])

    err, fac, igrad = call(
        finish_kernel,
        [((HEAD, WIDE), BF16), ((RANK, WIDE), BF16), ((OWN, WIDE), BF16)],
        flops=3 * 10**8,
        moved=5 * 10**6,
    )(mixed, right_other, basis, og, *acts, ef)

    return (err[None, None], basis.T[None], fac.T[None, None], igrad[None])


def solution(mesh):
    parted = Mesh(
        mesh.devices.reshape(4, 2, 4, 2, 4), EVERY
    )
    return jax.shard_map(
        local,
        mesh=parted,
        in_specs=(
            P(None, EVERY, None),
            P(None, DP, "t"),
            P(None, "t", None),
            P(None, DP, "t", None),
            P(None, "t", None, None),
        ),
        out_specs=(
            P(None, DP, "t", None),
            P(None, "t", None),
            P(None, "t", None, None),
            P(None, EVERY, None),
        ),
        check_vma=False,
    )
```

```python
import jax
import jax.numpy as jnp
from jax import lax
from jax.experimental import pallas as pl
from jax.experimental.pallas import tpu as pltpu
from jax.sharding import Mesh
from jax.sharding import PartitionSpec as P

F32 = jnp.float32
BF16 = jnp.bfloat16
HIGH = lax.Precision.HIGHEST
CHIPS = ("x", "zl", "y")
DP = ("x", "zl", "y", "core")
EVERY = DP + ("t",)

TENSOR = 4
REPLICAS = 64
WIDE = 4096
HEAD = 128
RANK = 32
HALF = RANK // 2
OWN = 32
CUT = 256
PLANE = 16
N_CHIPS = REPLICAS // 2
STEP = 512
NT = (((1,), (1,)), ((), ()))


def split3(x):
    hi = x.astype(BF16)
    rest = x - hi.astype(F32)
    mid = rest.astype(BF16)
    low = (rest - mid.astype(F32)).astype(BF16)
    return (hi, mid, low)


def split2(x):
    hi = x.astype(BF16)
    return (hi, (x - hi.astype(F32)).astype(BF16))


def turned(ref, t):
    blocks = [ref[pl.ds(((t - k + TENSOR) % TENSOR) * OWN, OWN), :] for k in range(TENSOR)]
    return jnp.concatenate(blocks, axis=0)


def call(kernel, outs, scratch=(), flops=10**6, moved=10**6, space=pltpu.VMEM, dest=pltpu.VMEM, room=8):

    def run(*args):
        return pl.pallas_call(
            kernel,
            out_shape=[jax.ShapeDtypeStruct(s, d) for s, d in outs],
            in_specs=[pl.BlockSpec(memory_space=space)] * len(args),
            out_specs=[pl.BlockSpec(memory_space=dest)] * len(outs),
            scratch_shapes=list(scratch),
            compiler_params=pltpu.CompilerParams(vmem_limit_bytes=room * 2**20),
            cost_estimate=pl.CostEstimate(flops=flops, bytes_accessed=moved, transcendentals=0),
        )(*args)

    return run


def fetched(pairs, sems):
    copies = [pltpu.make_async_copy(a, b, sems.at[i]) for i, (a, b) in enumerate(pairs)]
    for copy in copies:
        copy.start()
    for copy in copies:
        copy.wait()


def plane():
    return 4 * lax.axis_index("x") + lax.axis_index("y")


def pack_kernel(w, og, s1, s2, s3, feats, sems):
    t, core = lax.axis_index("t"), lax.axis_index("core")
    cols = pl.ds(pl.multiple_of(plane() * CUT, CUT), CUT)
    part = w.at[pl.ds(pl.multiple_of(core * 64, 64), 64), cols]
    sends = (s1, s2, s3)
    fetched([(part, s.at[pl.ds(0, 64), :]) for s in sends] + [(og, feats)], sems)
    for k, send in enumerate(sends, 1):
        first = OWN * lax.rem(t + k, TENSOR)
        for h in range(2):
            rows = pl.ds(pl.multiple_of(first + 16 * h, 16), 16)
            send[64:80, 128 * h : 128 * h + 128] = feats[rows, :]


def rows_kernel(og, r1, r2, r3, out, held):
    t = lax.axis_index("t")
    held[:, 0:128] = og[pl.ds(pl.multiple_of(OWN * t, OWN), OWN), :]
    for k, r in enumerate((r1, r2, r3), 1):
        for h in range(2):
            held[16 * h : 16 * h + 16, 128 * k : 128 * k + 128] = r[
                64:80, 128 * h : 128 * h + 128
            ]
    for g in range(PLANE):
        out[g] = held[...]


def early_kernel(a0, ef, warm, inner, fed, lines):
    lines[...] = warm[...]
    inner[...] = lax.dot_general(warm[...], a0[...], NT, preferred_element_type=F32)
    fed[...] = lax.dot_general(warm[...], ef[...], NT, preferred_element_type=F32)


def left_kernel(a1, a2, a3, og, lines, inner0, fed, keep, send, held):
    t, core = lax.axis_index("t"), lax.axis_index("core")
    ogp = turned(og, t)
    rest = [
        lax.dot_general(lines[...], a[...], NT, preferred_element_type=F32) for a in (a1, a2, a3)
    ]
    inner = jnp.concatenate([inner0[...]] + rest, axis=1)
    prod = jnp.dot(jnp.concatenate(split3(inner), axis=0), ogp, preferred_element_type=F32)
    held[...] = prod[0:RANK] + prod[RANK : 2 * RANK] + prod[2 * RANK :] + fed[...]
    keep[...] = held[pl.ds(pl.multiple_of(core * HALF, HALF), HALF), :]
    send[...] = held[pl.ds(pl.multiple_of((1 - core) * HALF, HALF), HALF), :]


def basis_kernel(lown, loth, a0, a1, a2, a3, og, ef, qt, keep, send, held, heldo):
    t, core = lax.axis_index("t"), lax.axis_index("core")
    mine = pl.ds(pl.multiple_of(core * HALF, HALF), HALF)
    other = pl.ds(pl.multiple_of((1 - core) * HALF, HALF), HALF)
    held[mine, :] = lown[...]
    held[other, :] = loth[...]
    left = held[...]
    gram = lax.dot_general(left, left, NT, precision=HIGH, preferred_element_type=F32)
    row = lax.broadcasted_iota(jnp.int32, (RANK, 1), 0)
    for k in range(0, RANK, 2):
        first_g, first_l = gram[k : k + 1, :], left[k : k + 1, :]
        corner = gram[k : k + 1, k + 1 : k + 2]
        scale = 1.0 / gram[k : k + 1, k : k + 1]
        ratio = corner * scale
        pivot = 1.0 / (gram[k + 1 : k + 2, k + 1 : k + 2] - ratio * corner)
        column = gram[:, k : k + 1]
        one = jnp.where(row > k, column * scale, 0.0)
        two = jnp.where(row > k + 1, (gram[:, k + 1 : k + 2] - column * ratio) * pivot, 0.0)
        second_g = gram[k + 1 : k + 2, :] - ratio * first_g
        second_l = left[k + 1 : k + 2, :] - ratio * first_l
        gram = gram - one * first_g - two * second_g
        left = left - one * first_l - two * second_l
    eye = row == lax.broadcasted_iota(jnp.int32, (RANK, RANK), 1)
    diagonal = jnp.sum(jnp.where(eye, gram, 0.0), axis=1, keepdims=True)
    basis = left * (1.0 / jnp.sqrt(diagonal))
    qt[...] = basis
    ogp = turned(og, t)
    prod = lax.dot_general(
        jnp.concatenate(split3(basis), axis=0), ogp, NT, preferred_element_type=F32
    )
    held[...] = basis
    heldo[...] = prod[0:RANK] + prod[RANK : 2 * RANK] + prod[2 * RANK :]
    q = jnp.concatenate([held[mine, :], held[other, :]], axis=0)
    qo = jnp.concatenate([heldo[mine, :], heldo[other, :]], axis=0)
    lhs = jnp.concatenate(
        [jnp.concatenate(split3(qo), axis=0), jnp.concatenate(split3(q), axis=0)], axis=1
    )
    for c in range(0, WIDE, STEP):
        cols = slice(c, c + STEP)
        rhs = jnp.concatenate([a[:, cols] for a in (a0, a1, a2, a3, ef)], axis=0)
        p = jnp.dot(lhs, rhs, preferred_element_type=F32)
        r = p[0:RANK] + p[RANK : 2 * RANK] + p[2 * RANK :]
        for j in range(STEP // 128):
            chip = c // 128 + j
            keep[chip] = r[0:HALF, 128 * j : 128 * j + 128]
            send[chip] = r[HALF:, 128 * j : 128 * j + 128]


def spread_kernel(pieces, inputs, out):
    hi, mid = split2(jnp.sum(pieces[...], axis=0) * (1.0 / REPLICAS))
    for chip in range(N_CHIPS):
        g = chip // 8 * 4 + chip % 4
        out[chip, 0:16, :] = hi
        out[chip, 16:32, :] = mid
        out[chip, 32:64, :] = inputs[g, :, 0:128]
        out[chip, 64:96, :] = inputs[g, :, 128:256]


def finish_kernel(mixed, roth, qt, og, a0, a1, a2, a3, ef, err, fac, igrad):
    t, core = lax.axis_index("t"), lax.axis_index("core")
    zl = lax.axis_index("zl")
    mine = pl.ds(pl.multiple_of(core * HALF, HALF), HALF)
    other = pl.ds(pl.multiple_of((1 - core) * HALF, HALF), HALF)
    for g in range(PLANE):
        chip = g // 4 * 8 + 4 * zl + g % 4
        igrad[:, CUT * g : CUT * g + 128] = mixed[chip, 32:64, :]
        igrad[:, CUT * g + 128 : CUT * g + 256] = mixed[chip, 64:96, :]
    q = jnp.concatenate([qt[mine, :], qt[other, :]], axis=0)
    hi, mid = split2(q)
    hi, mid = hi.astype(F32), mid.astype(F32)
    ogp = turned(og, t).astype(F32)
    lhs = jnp.concatenate([ogp, -hi, -hi, -mid, -mid], axis=0).T.astype(BF16)
    for c in range(0, WIDE, STEP):
        cols = slice(c, c + STEP)
        chips = range(c // 128, (c + STEP) // 128)
        own = jnp.concatenate([mixed[j, 0:32, :] for j in chips], axis=1)
        oth = jnp.concatenate([roth[j] for j in chips], axis=1)
        fac[mine, cols] = own[0:16]
        fac[other, cols] = oth[0:16]
        high = jnp.concatenate([own[0:16], oth[0:16]], axis=0)
        low = jnp.concatenate([own[16:32], oth[16:32]], axis=0)
        rhs = jnp.concatenate(
            [a[:, cols] for a in (a0, a1, a2, a3)] + [high, low, high, low], axis=0
        )
        total = jnp.dot(lhs, rhs, preferred_element_type=F32) + ef[:, cols].astype(F32)
        err[:, cols] = total.astype(BF16)


def input_kernel(w, feats, r1, r2, r3, c1, c2, c3, out, fv, weights, total, sems):
    core = lax.axis_index("core")
    cols = pl.ds(pl.multiple_of(plane() * CUT, CUT), CUT)
    pairs = [(w.at[:, cols], weights.at[pl.ds(0, HEAD), :]), (feats, fv)]
    for k, (r, c) in enumerate(((r1, c1), (r2, c2), (r3, c3)), 1):
        for source, side in ((r, core), (c, 1 - core)):
            rows = pl.ds(pl.multiple_of(HEAD * k + 64 * side, 64), 64)
            pairs.append((source.at[pl.ds(0, 64), :], weights.at[rows, :]))
    fetched(pairs, sems)
    for g in range(0, PLANE, 4):
        rows = jnp.concatenate([fv[g + i] for i in range(4)], axis=0)
        part = jnp.dot(rows, weights[...], preferred_element_type=F32).astype(BF16)
        for i in range(4):
            total[g + i] = part[OWN * i : OWN * i + OWN]
    fetched([(total, out)], sems)


def moved(x, k, axis="t"):
    return lax.ppermute(x, axis, [(i, (i + k) % 4) for i in range(4)])


def swapped(x):
    return lax.ppermute(x, "core", [(0, 1), (1, 0)])


def exchanged(x, axes):
    return lax.all_to_all(x, axes, 0, 0, tiled=True)


def local(activations, out_grad, value_weight, error_feedback, warm_right):
    act, og, weight = activations[0], out_grad[0], value_weight[0]
    ef = error_feedback[0, 0]
    warm = warm_right[0, 0].T

    sends = call(
        pack_kernel,
        [((80, CUT), BF16)] * 3,
        [pltpu.VMEM((128, HEAD), BF16), pltpu.SemaphoreType.DMA((4,))],
        space=pltpu.MemorySpace.HBM,
        room=60,
    )(weight, og)
    got = [moved(x, k) for k, x in zip((1, 2, 3), sends)]
    acts = [act] + [moved(act, k) for k in (1, 2, 3)]
    (rows,) = call(rows_kernel, [((PLANE, OWN, 512), BF16)], [pltpu.VMEM((OWN, 512), BF16)])(og, *got)
    feats = exchanged(rows, ("x", "y"))
    inner, fed, lines = call(
        early_kernel,
        [((RANK, OWN), F32), ((RANK, HEAD), F32), ((RANK, WIDE), BF16)],
        flops=10**10,
        moved=10**8,
    )(act, ef, warm)

    got, inner = lax.optimization_barrier((got, inner))
    traded = [swapped(g) for g in got]
    (inputs,) = call(
        input_kernel,
        [((PLANE, OWN, CUT), BF16)],
        [
            pltpu.VMEM((PLANE, OWN, 512), BF16),
            pltpu.VMEM((512, CUT), BF16),
            pltpu.VMEM((PLANE, OWN, CUT), BF16),
            pltpu.SemaphoreType.DMA((8,)),
        ],
        flops=2 * 10**8,
        moved=2 * 10**6,
        space=pltpu.MemorySpace.HBM,
        dest=pltpu.MemorySpace.HBM,
        room=60,
    )(weight, feats, *got, *traded)
    lines, inputs = lax.optimization_barrier((lines, inputs))
    half = ((HALF, HEAD), F32)
    left_keep, left_send = call(
        left_kernel, [half, half], [pltpu.VMEM((RANK, HEAD), F32)], flops=5 * 10**7, moved=10**6
    )(*acts[1:], og, lines, inner, fed)

    left_half = left_keep + swapped(left_send)
    pieces = exchanged(jnp.broadcast_to(left_half[None], (N_CHIPS, HALF, HEAD)), CHIPS)
    left_own = jnp.sum(pieces, axis=0)
    left_other = swapped(left_own)

    block = ((N_CHIPS, HALF, 128), F32)
    basis, right_keep, right_send = call(
        basis_kernel,
        [((RANK, HEAD), F32), block, block],
        [pltpu.VMEM((RANK, HEAD), F32), pltpu.VMEM((RANK, HEAD), F32)],
        flops=10**8,
        moved=3 * 10**6,
    )(left_own, left_other, *acts, og, ef)

    pieces = exchanged(right_keep + swapped(right_send), CHIPS)
    (mixed,) = call(spread_kernel, [((N_CHIPS, 96, 128), BF16)])(pieces, inputs)
    mixed = exchanged(mixed, CHIPS)
    right_other = swapped(mixed[:, 0:32])

    err, fac, igrad = call(
        finish_kernel,
        [((HEAD, WIDE), BF16), ((RANK, WIDE), BF16), ((OWN, WIDE), BF16)],
        flops=3 * 10**8,
        moved=5 * 10**6,
    )(mixed, right_other, basis, og, *acts, ef)

    return (err[None, None], basis.T[None], fac.T[None, None], igrad[None])


def solution(mesh):
    parted = Mesh(
        mesh.devices.reshape(4, 2, 4, 2, 4), EVERY
    )
    return jax.shard_map(
        local,
        mesh=parted,
        in_specs=(
            P(None, EVERY, None),
            P(None, DP, "t"),
            P(None, "t", None),
            P(None, DP, "t", None),
            P(None, "t", None, None),
        ),
        out_specs=(
            P(None, DP, "t", None),
            P(None, "t", None),
            P(None, "t", None, None),
            P(None, EVERY, None),
        ),
        check_vma=False,
    )
```

```python
import jax
import jax.numpy as jnp
from jax import lax
from jax.experimental import pallas as pl
from jax.experimental.pallas import tpu as pltpu
from jax.sharding import Mesh
from jax.sharding import PartitionSpec as P

F32 = jnp.float32
BF16 = jnp.bfloat16
HIGH = lax.Precision.HIGHEST
CHIPS = ("x", "zl", "y")
DP = ("x", "zl", "y", "core")
EVERY = DP + ("t",)

TENSOR = 4
REPLICAS = 64
WIDE = 4096
HEAD = 128
RANK = 32
HALF = RANK // 2
OWN = 32
CUT = 256
PLANE = 16
N_CHIPS = REPLICAS // 2
STEP = 512
NT = (((1,), (1,)), ((), ()))


def split3(x):
    hi = x.astype(BF16)
    rest = x - hi.astype(F32)
    mid = rest.astype(BF16)
    low = (rest - mid.astype(F32)).astype(BF16)
    return (hi, mid, low)


def split2(x):
    hi = x.astype(BF16)
    return (hi, (x - hi.astype(F32)).astype(BF16))


def turned(ref, t):
    blocks = [ref[pl.ds(((t - k + TENSOR) % TENSOR) * OWN, OWN), :] for k in range(TENSOR)]
    return jnp.concatenate(blocks, axis=0)


def call(kernel, outs, scratch=(), flops=10**6, moved=10**6, space=pltpu.VMEM, dest=pltpu.VMEM, room=8):

    def run(*args):
        return pl.pallas_call(
            kernel,
            out_shape=[jax.ShapeDtypeStruct(s, d) for s, d in outs],
            in_specs=[pl.BlockSpec(memory_space=space)] * len(args),
            out_specs=[pl.BlockSpec(memory_space=dest)] * len(outs),
            scratch_shapes=list(scratch),
            compiler_params=pltpu.CompilerParams(vmem_limit_bytes=room * 2**20),
            cost_estimate=pl.CostEstimate(flops=flops, bytes_accessed=moved, transcendentals=0),
        )(*args)

    return run


def fetched(pairs, sems):
    copies = [pltpu.make_async_copy(a, b, sems.at[i]) for i, (a, b) in enumerate(pairs)]
    for copy in copies:
        copy.start()
    for copy in copies:
        copy.wait()


def plane():
    return 4 * lax.axis_index("x") + lax.axis_index("y")


def pack_kernel(w, og, s1, s2, s3, feats, sems):
    t, core = lax.axis_index("t"), lax.axis_index("core")
    cols = pl.ds(pl.multiple_of(plane() * CUT, CUT), CUT)
    part = w.at[pl.ds(pl.multiple_of(core * 64, 64), 64), cols]
    sends = (s1, s2, s3)
    fetched([(part, s.at[pl.ds(0, 64), :]) for s in sends] + [(og, feats)], sems)
    for k, send in enumerate(sends, 1):
        first = OWN * lax.rem(t + k, TENSOR)
        for h in range(2):
            rows = pl.ds(pl.multiple_of(first + 16 * h, 16), 16)
            send[64:80, 128 * h : 128 * h + 128] = feats[rows, :]


def rows_kernel(og, r1, r2, r3, out, held):
    t = lax.axis_index("t")
    held[:, 0:128] = og[pl.ds(pl.multiple_of(OWN * t, OWN), OWN), :]
    for k, r in enumerate((r1, r2, r3), 1):
        for h in range(2):
            held[16 * h : 16 * h + 16, 128 * k : 128 * k + 128] = r[
                64:80, 128 * h : 128 * h + 128
            ]
    for g in range(PLANE):
        out[g] = held[...]


def early_kernel(a0, ef, warm, inner, fed, lines):
    lines[...] = warm[...]
    inner[...] = lax.dot_general(warm[...], a0[...], NT, preferred_element_type=F32)
    fed[...] = lax.dot_general(warm[...], ef[...], NT, preferred_element_type=F32)


def left_kernel(a1, a2, a3, og, lines, inner0, fed, keep, send, held):
    t, core = lax.axis_index("t"), lax.axis_index("core")
    ogp = turned(og, t)
    rest = [
        lax.dot_general(lines[...], a[...], NT, preferred_element_type=F32) for a in (a1, a2, a3)
    ]
    inner = jnp.concatenate([inner0[...]] + rest, axis=1)
    prod = jnp.dot(jnp.concatenate(split3(inner), axis=0), ogp, preferred_element_type=F32)
    held[...] = prod[0:RANK] + prod[RANK : 2 * RANK] + prod[2 * RANK :] + fed[...]
    keep[...] = held[pl.ds(pl.multiple_of(core * HALF, HALF), HALF), :]
    send[...] = held[pl.ds(pl.multiple_of((1 - core) * HALF, HALF), HALF), :]


def basis_kernel(lown, loth, a0, a1, a2, a3, og, ef, qt, keep, send, held, heldo):
    t, core = lax.axis_index("t"), lax.axis_index("core")
    mine = pl.ds(pl.multiple_of(core * HALF, HALF), HALF)
    other = pl.ds(pl.multiple_of((1 - core) * HALF, HALF), HALF)
    held[mine, :] = lown[...]
    held[other, :] = loth[...]
    left = held[...]
    gram = lax.dot_general(left, left, NT, precision=HIGH, preferred_element_type=F32)
    row = lax.broadcasted_iota(jnp.int32, (RANK, 1), 0)
    for k in range(RANK - 1):
        scale = 1.0 / gram[k : k + 1, k : k + 1]
        factor = jnp.where(row > k, gram[:, k : k + 1], 0.0) * scale
        pivot_g, pivot_l = gram[k : k + 1, :], left[k : k + 1, :]
        gram = gram - factor * pivot_g
        left = left - factor * pivot_l
    eye = row == lax.broadcasted_iota(jnp.int32, (RANK, RANK), 1)
    diagonal = jnp.sum(jnp.where(eye, gram, 0.0), axis=1, keepdims=True)
    basis = left * (1.0 / jnp.sqrt(diagonal))
    qt[...] = basis
    ogp = turned(og, t)
    prod = lax.dot_general(
        jnp.concatenate(split3(basis), axis=0), ogp, NT, preferred_element_type=F32
    )
    held[...] = basis
    heldo[...] = prod[0:RANK] + prod[RANK : 2 * RANK] + prod[2 * RANK :]
    q = jnp.concatenate([held[mine, :], held[other, :]], axis=0)
    qo = jnp.concatenate([heldo[mine, :], heldo[other, :]], axis=0)
    lhs = jnp.concatenate(
        [jnp.concatenate(split3(qo), axis=0), jnp.concatenate(split3(q), axis=0)], axis=1
    )
    for c in range(0, WIDE, STEP):
        cols = slice(c, c + STEP)
        rhs = jnp.concatenate([a[:, cols] for a in (a0, a1, a2, a3, ef)], axis=0)
        p = jnp.dot(lhs, rhs, preferred_element_type=F32)
        r = p[0:RANK] + p[RANK : 2 * RANK] + p[2 * RANK :]
        for j in range(STEP // 128):
            chip = c // 128 + j
            keep[chip] = r[0:HALF, 128 * j : 128 * j + 128]
            send[chip] = r[HALF:, 128 * j : 128 * j + 128]


def spread_kernel(pieces, inputs, out):
    hi, mid = split2(jnp.sum(pieces[...], axis=0) * (1.0 / REPLICAS))
    for chip in range(N_CHIPS):
        g = chip // 8 * 4 + chip % 4
        out[chip, 0:16, :] = hi
        out[chip, 16:32, :] = mid
        out[chip, 32:64, :] = inputs[g, :, 0:128]
        out[chip, 64:96, :] = inputs[g, :, 128:256]


def finish_kernel(mixed, roth, qt, og, a0, a1, a2, a3, ef, err, fac, igrad):
    t, core = lax.axis_index("t"), lax.axis_index("core")
    zl = lax.axis_index("zl")
    mine = pl.ds(pl.multiple_of(core * HALF, HALF), HALF)
    other = pl.ds(pl.multiple_of((1 - core) * HALF, HALF), HALF)
    for g in range(PLANE):
        chip = g // 4 * 8 + 4 * zl + g % 4
        igrad[:, CUT * g : CUT * g + 128] = mixed[chip, 32:64, :]
        igrad[:, CUT * g + 128 : CUT * g + 256] = mixed[chip, 64:96, :]
    q = jnp.concatenate([qt[mine, :], qt[other, :]], axis=0)
    hi, mid = split2(q)
    hi, mid = hi.astype(F32), mid.astype(F32)
    ogp = turned(og, t).astype(F32)
    lhs = jnp.concatenate([ogp, -hi, -hi, -mid, -mid], axis=0).T.astype(BF16)
    for c in range(0, WIDE, STEP):
        cols = slice(c, c + STEP)
        chips = range(c // 128, (c + STEP) // 128)
        own = jnp.concatenate([mixed[j, 0:32, :] for j in chips], axis=1)
        oth = jnp.concatenate([roth[j] for j in chips], axis=1)
        fac[mine, cols] = own[0:16]
        fac[other, cols] = oth[0:16]
        high = jnp.concatenate([own[0:16], oth[0:16]], axis=0)
        low = jnp.concatenate([own[16:32], oth[16:32]], axis=0)
        rhs = jnp.concatenate(
            [a[:, cols] for a in (a0, a1, a2, a3)] + [high, low, high, low], axis=0
        )
        total = jnp.dot(lhs, rhs, preferred_element_type=F32) + ef[:, cols].astype(F32)
        err[:, cols] = total.astype(BF16)


def input_kernel(w, feats, r1, r2, r3, c1, c2, c3, out, fv, weights, total, sems):
    core = lax.axis_index("core")
    cols = pl.ds(pl.multiple_of(plane() * CUT, CUT), CUT)
    pairs = [(w.at[:, cols], weights.at[pl.ds(0, HEAD), :]), (feats, fv)]
    for k, (r, c) in enumerate(((r1, c1), (r2, c2), (r3, c3)), 1):
        for source, side in ((r, core), (c, 1 - core)):
            rows = pl.ds(pl.multiple_of(HEAD * k + 64 * side, 64), 64)
            pairs.append((source.at[pl.ds(0, 64), :], weights.at[rows, :]))
    fetched(pairs, sems)
    for g in range(0, PLANE, 4):
        rows = jnp.concatenate([fv[g + i] for i in range(4)], axis=0)
        part = jnp.dot(rows, weights[...], preferred_element_type=F32).astype(BF16)
        for i in range(4):
            total[g + i] = part[OWN * i : OWN * i + OWN]
    fetched([(total, out)], sems)


def moved(x, k, axis="t"):
    return lax.ppermute(x, axis, [(i, (i + k) % 4) for i in range(4)])


def swapped(x):
    return lax.ppermute(x, "core", [(0, 1), (1, 0)])


def exchanged(x, axes):
    return lax.all_to_all(x, axes, 0, 0, tiled=True)


def local(activations, out_grad, value_weight, error_feedback, warm_right):
    act, og, weight = activations[0], out_grad[0], value_weight[0]
    ef = error_feedback[0, 0]
    warm = warm_right[0, 0].T

    sends = call(
        pack_kernel,
        [((80, CUT), BF16)] * 3,
        [pltpu.VMEM((128, HEAD), BF16), pltpu.SemaphoreType.DMA((4,))],
        space=pltpu.MemorySpace.HBM,
        room=60,
    )(weight, og)
    got = [moved(x, k) for k, x in zip((1, 2, 3), sends)]
    acts = [act] + [moved(act, k) for k in (1, 2, 3)]
    (rows,) = call(rows_kernel, [((PLANE, OWN, 512), BF16)], [pltpu.VMEM((OWN, 512), BF16)])(og, *got)
    feats = exchanged(rows, ("x", "y"))
    inner, fed, lines = call(
        early_kernel,
        [((RANK, OWN), F32), ((RANK, HEAD), F32), ((RANK, WIDE), BF16)],
        flops=10**10,
        moved=10**8,
    )(act, ef, warm)

    got, inner = lax.optimization_barrier((got, inner))
    traded = [swapped(g) for g in got]
    (inputs,) = call(
        input_kernel,
        [((PLANE, OWN, CUT), BF16)],
        [
            pltpu.VMEM((PLANE, OWN, 512), BF16),
            pltpu.VMEM((512, CUT), BF16),
            pltpu.VMEM((PLANE, OWN, CUT), BF16),
            pltpu.SemaphoreType.DMA((8,)),
        ],
        flops=2 * 10**8,
        moved=2 * 10**6,
        space=pltpu.MemorySpace.HBM,
        dest=pltpu.MemorySpace.HBM,
        room=60,
    )(weight, feats, *got, *traded)
    lines, inputs = lax.optimization_barrier((lines, inputs))
    half = ((HALF, HEAD), F32)
    left_keep, left_send = call(
        left_kernel, [half, half], [pltpu.VMEM((RANK, HEAD), F32)], flops=5 * 10**7, moved=10**6
    )(*acts[1:], og, lines, inner, fed)

    left_half = left_keep + swapped(left_send)
    pieces = exchanged(jnp.broadcast_to(left_half[None], (N_CHIPS, HALF, HEAD)), CHIPS)
    left_own = jnp.sum(pieces, axis=0)
    left_other = swapped(left_own)

    block = ((N_CHIPS, HALF, 128), F32)
    basis, right_keep, right_send = call(
        basis_kernel,
        [((RANK, HEAD), F32), block, block],
        [pltpu.VMEM((RANK, HEAD), F32), pltpu.VMEM((RANK, HEAD), F32)],
        flops=10**8,
        moved=3 * 10**6,
    )(left_own, left_other, *acts, og, ef)

    pieces = exchanged(right_keep + swapped(right_send), CHIPS)
    (mixed,) = call(spread_kernel, [((N_CHIPS, 96, 128), BF16)])(pieces, inputs)
    mixed = exchanged(mixed, CHIPS)
    right_other = swapped(mixed[:, 0:32])

    err, fac, igrad = call(
        finish_kernel,
        [((HEAD, WIDE), BF16), ((RANK, WIDE), BF16), ((OWN, WIDE), BF16)],
        flops=3 * 10**8,
        moved=5 * 10**6,
    )(mixed, right_other, basis, og, *acts, ef)

    return (err[None, None], basis.T[None], fac.T[None, None], igrad[None])


def solution(mesh):
    parted = Mesh(
        mesh.devices.reshape(4, 2, 4, 2, 4), EVERY
    )
    return jax.shard_map(
        local,
        mesh=parted,
        in_specs=(
            P(None, EVERY, None),
            P(None, DP, "t"),
            P(None, "t", None),
            P(None, DP, "t", None),
            P(None, "t", None, None),
        ),
        out_specs=(
            P(None, DP, "t", None),
            P(None, "t", None),
            P(None, "t", None, None),
            P(None, EVERY, None),
        ),
        check_vma=False,
    )
```
